256 devices in a mesh: comp: 2 (over x_lo), panel: 4 (over x_hi, core), col: 32 (over z, y).
Axes of the slice: x: 4 (x_hi: 2, x_lo: 2; x = x_hi * 2 + x_lo), y: 4, z: 8, core: 2. Of those that a mesh axis runs over, the one named last changes fastest.
Arguments:
- joint_tracer_field: float32 [2, 2, 4, 2048, 1024], P('comp', None, None, 'col', 'panel'), may hold values from -5 to 5
- courant_mixing_rates: float32 [2, 3, 4, 2048, 1024], P('comp', None, None, 'col', 'panel'), may hold values from -0.24 to 0.24, as said below
- oceanic_indicator: int32 [2, 2048, 1024], P('comp', 'col', 'panel'), may hold values 0 or 1
- glacial_indicator: int32 [2048, 1024], P('col', 'panel'), may hold values 0 or 1
- prior_oceanic_warmth: float32 [2048, 1024], P('col', 'panel'), may hold values from -4 to 4
- prior_glacial_cover: float32 [2048, 1024], P('col', 'panel'), may hold values from 0 to 0.8
- partner_devices: int32 [16384, 2], P(('panel', 'col')), may hold values from 0 to 127, all different within a row; in each aligned block of 128 rows (0 to 127, 128 to 255, ...) at most 4 rows name the same one
- receiving_tile_index: int32 [16384, 2], P(('panel', 'col')), may hold values from 0 to 127
- bank_tile_entry: int32 [16384, 2], P(('panel', 'col')), may hold values from 0 to 31
- conservative_overlay_factors: float32 [32, 128, 128], replicated, may hold values from 0.002 to 0.014
Outputs:
- new_state: float32 [2, 2, 4, 2048, 1024], P('comp', None, None, 'col', 'panel')
- surface: float32 [2, 2, 2048, 1024], P('comp', None, 'col', 'panel')
The draws below stay inside these ranges and needn't reach their ends.
Inputs may be any that keep to these rules, and one draw needn't show every extreme that they name: `partner_devices`: each row names two different ocean devices, device p * 32 + q lying at index p of panel and q of col. Among the 128 rows of one device no ocean device is named more than 4 times, and in the rows of some devices one is named exactly 4 times. courant_mixing_rates[c, 0] and courant_mixing_rates[c, 1] lie in [-0.24, 0.24]; courant_mixing_rates[c, 2] lies in [0.01, 0.24].
All inputs are finite; a program needn't handle non-finite values. No bound on the sum of `oceanic_indicator` or of `glacial_indicator` on one device may be relied on, other than what follows from the above.
Results may differ from the reference program's by a relative error of at most 0.00013.
Values sent between devices are 32-bit elements; how exact they have to be, the bound alone decides.
A program may use at most 64 MiB of HBM per device.

```python
import math
import jax
import jax.numpy as jnp
import numpy as np
from jax import lax

CY = 64
CX = 256
TILE = 128
LEV = 4
NSUB = 4
NBANK = 32
MERIDIONAL_COUNT = 2048
ZONAL_COUNT = 1024
ATILE_DEV = 128
ATILES = 16384
CAP = 4
N_PANEL = 4
N_COL = 32


def draw_courant_mixing_rates(key, part):
    key_vel, key_mix = jax.random.split(key)
    velocity = jax.random.uniform(key_vel, (2, 2, LEV, MERIDIONAL_COUNT, ZONAL_COUNT), jnp.float32, -0.24, 0.24)
    mixing = jnp.exp(jax.random.uniform(key_mix, (2, 1, LEV, MERIDIONAL_COUNT, ZONAL_COUNT), jnp.float32, math.log(0.01), math.log(0.24)))
    return jnp.concatenate([velocity, mixing], axis=1)


def set_ends(entries, own_key, low, top_value):
    longest = entries.shape.index(max(entries.shape))
    spots = []
    for shift in (0, 1):
        where = [jax.random.randint(jax.random.fold_in(own_key, axis), (), 0, length) for axis, length in enumerate(entries.shape)]
        where[longest] = (where[longest] + shift) % entries.shape[longest]
        spots.append(tuple(where))
    return entries.at[spots[0]].set(low).at[spots[1]].set(top_value)


def level_of(stream_key, dims, cuts, smallest, top_value):
    def one(position, parts):
        steps = jax.random.uniform(jax.random.fold_in(jax.random.fold_in(stream_key, 6), position), (parts,), jnp.float32, smallest / len(cuts), top_value / len(cuts))
        return jnp.repeat(jnp.exp(steps), dims[position] // parts).reshape((-1,) + (1,) * (len(dims) - position - 1))

    level = one(*cuts[0])
    for cut in cuts[1:]:
        level = level * one(*cut)
    return level


def deal_out(own_key, own, number, rows, number_of, top, limit, lean):
    order = jax.random.permutation(own_key, number_of)
    packed, ordinary = shares(number_of, rows * top, limit, lean, True), shares(number_of, rows * top, limit, lean, False)
    places = jnp.arange(number_of)

    def named(sizes, turn):
        used = int((sizes > 0).sum())
        fixed = max(1, used // 4)
        moved = fixed + (places - fixed + turn * (used - fixed)) % max(1, number_of - fixed)
        return jnp.zeros((number_of,), jnp.int32).at[order[jnp.where(places < fixed, places, moved)]].set(jnp.asarray(sizes, jnp.int32))

    sizes = jnp.where(number % 4 == 0, named(packed, number // 4), named(ordinary, number - number // 4 - 1))
    mixed = jax.random.permutation(jax.random.fold_in(own, 3), number_of)
    giver, sink = mixed[0:number_of // 2 * 2:2], mixed[1:number_of // 2 * 2:2]
    room = jnp.minimum(sizes[giver] - 1, limit - sizes[sink]) // 2
    room = jnp.where((giver == order[0]) | (sink == order[0]) | (sizes[sink] == 0), 0, jnp.maximum(room, 0))
    moved = jax.random.randint(jax.random.fold_in(own, 4), (number_of // 2,), 0, 1 << 20) % (room + 1)
    sizes = sizes.at[giver].add(-moved).at[sink].add(moved)
    labels = jnp.searchsorted(jnp.cumsum(sizes), jnp.arange(rows * top), side="right").astype(jnp.int32)
    grid = labels.reshape(top, rows).T
    grid = grid[jax.random.permutation(jax.random.fold_in(own, 1), rows)]
    turn = jax.random.randint(jax.random.fold_in(own, 2), (rows, 1), 0, top)
    return jnp.take_along_axis(grid, (jnp.arange(top)[None, :] + turn) % top, axis=1)


def shares(number_of, total, limit, slope, full):
    weights = [(1 << 20) // math.isqrt(grade ** slope) + 1 for grade in range(1, number_of + 1)]
    largest = limit if full else min(limit, max(-(-total // number_of), total * weights[0] // sum(weights)))
    least = 1 if total - largest >= number_of - 1 else 0
    holding, spare = [largest] + [least] * (number_of - 1), total - largest - least * (number_of - 1)
    while spare > 0:
        free = [i for i in range(1, number_of) if holding[i] < largest] or [i for i in range(1, number_of) if holding[i] < limit]
        whole, budget = sum([weights[i] for i in free]), spare
        for i in free:
            more = min(limit - holding[i], max(1, budget * weights[i] // whole), spare)
            holding[i] = holding[i] + more
            spare = spare - more
    return np.array(holding)


def scatter_about(key, dims, deviation, most, cuts=(), held_as=jnp.bfloat16):
    values = jax.random.normal(key, dims, jnp.float32) * deviation
    if len(cuts) > 0:
        values = level_of(key, dims, cuts, -0.22, 0.18) * values
    return jnp.clip(values, min=-most, max=most).astype(held_as)


def setup_inputs(seed: int = 0) -> dict:
    arg_keys = jax.random.split(jax.random.key(seed), 11)
    joint_tracer_field = scatter_about(arg_keys[0], (2, 2, LEV, MERIDIONAL_COUNT, ZONAL_COUNT), 1.0, 5.0, ((0, 2), (3, 32), (4, 4)), jnp.float32)
    courant_mixing_rates = draw_courant_mixing_rates(jax.random.fold_in(arg_keys[10], 71), 0)
    oceanic_indicator = set_ends((jax.random.randint(arg_keys[2], (2, MERIDIONAL_COUNT, ZONAL_COUNT), 0, 4) < 3).astype(jnp.int32), jax.random.fold_in(arg_keys[2], 1), 0, 1)
    glacial_indicator = set_ends((jax.random.randint(arg_keys[3], (MERIDIONAL_COUNT, ZONAL_COUNT), 0, 2) < 1).astype(jnp.int32), jax.random.fold_in(arg_keys[3], 1), 0, 1)
    prior_oceanic_warmth = scatter_about(arg_keys[4], (MERIDIONAL_COUNT, ZONAL_COUNT), 1.0, 4.0, ((0, 32), (1, 4)), jnp.float32)
    prior_glacial_cover = jnp.clip(0.8 * jax.random.uniform(arg_keys[5], (MERIDIONAL_COUNT, ZONAL_COUNT), jnp.float32) ** level_of(arg_keys[5], (MERIDIONAL_COUNT, ZONAL_COUNT), ((0, 32), (1, 4)), -0.2, 0.2), 0.0, 0.8)
    partner_devices_keys = jax.random.split(jax.random.fold_in(arg_keys[6], 1), ATILES // ATILE_DEV)
    partner_devices_turns = jax.random.permutation(jax.random.fold_in(arg_keys[6], 3), ATILES // ATILE_DEV)
    partner_devices = jax.vmap(lambda own, number: deal_out(jax.random.fold_in(arg_keys[6], 2), own, number, ATILE_DEV, N_PANEL * N_COL, 2, CAP, 2))(partner_devices_keys, partner_devices_turns).reshape((ATILES, 2))
    receiving_tile_index = set_ends(jax.random.randint(arg_keys[7], (ATILES, 2), 0, ATILE_DEV), jax.random.fold_in(arg_keys[7], 1), 0, ATILE_DEV - 1).astype(jnp.int32)
    bank_tile_entry = set_ends(jax.random.randint(arg_keys[8], (ATILES, 2), 0, NBANK), jax.random.fold_in(arg_keys[8], 1), 0, NBANK - 1).astype(jnp.int32)
    conservative_overlay_factors = jnp.clip(jax.random.uniform(arg_keys[9], (NBANK, TILE, TILE), jnp.float32, 0.002, 0.014), 0.002, 0.014)
    return dict(joint_tracer_field=joint_tracer_field, courant_mixing_rates=courant_mixing_rates, oceanic_indicator=oceanic_indicator, glacial_indicator=glacial_indicator, prior_oceanic_warmth=prior_oceanic_warmth, prior_glacial_cover=prior_glacial_cover, partner_devices=partner_devices, receiving_tile_index=receiving_tile_index, bank_tile_entry=bank_tile_entry, conservative_overlay_factors=conservative_overlay_factors)


def vertical_mix(tracer, mixing):
    level_flux = mixing[:-1] * (tracer[:, 1:] - tracer[:, :-1])
    zero_level = jnp.zeros_like(tracer[:, :1])
    from_above = jnp.concatenate([level_flux, zero_level], axis=1)
    from_below = jnp.concatenate([zero_level, level_flux], axis=1)
    relaxation = jnp.concatenate([jnp.zeros_like(tracer[:, :-1]), mixing[-1:] * tracer[:, -1:]], axis=1)
    return tracer + from_above - from_below - relaxation

def advect_mix(tracer, east_vel, north_vel, mixing):
    centre = tracer[..., 1:-1, 1:-1]
    vel_east = east_vel[:, 1:-1, 1:-1]
    vel_west = east_vel[:, 1:-1, :-2]
    vel_north = north_vel[:, 1:-1, 1:-1]
    vel_south = north_vel[:, :-2, 1:-1]
    flux_east = jnp.maximum(vel_east, 0.0) * centre + jnp.minimum(vel_east, 0.0) * tracer[..., 1:-1, 2:]
    flux_west = jnp.maximum(vel_west, 0.0) * tracer[..., 1:-1, :-2] + jnp.minimum(vel_west, 0.0) * centre
    flux_north = jnp.maximum(vel_north, 0.0) * centre + jnp.minimum(vel_north, 0.0) * tracer[..., 2:, 1:-1]
    flux_south = jnp.maximum(vel_south, 0.0) * tracer[..., :-2, 1:-1] + jnp.minimum(vel_south, 0.0) * centre
    advanced = centre - (flux_east - flux_west) - (flux_north - flux_south)
    return vertical_mix(advanced, mixing[:, 1:-1, 1:-1])

def extend_grid(field_grid):
    lead = [(0, 0)] * (field_grid.ndim - 2)
    padded = jnp.pad(field_grid, lead + [(1, 1), (0, 0)])
    return jnp.pad(padded, lead + [(0, 0), (1, 1)], mode='wrap')

def grid_to_tiles(field_grid):
    fcount = field_grid.shape[0]
    blocks = field_grid.reshape(fcount, N_COL, CY, N_PANEL, CX // TILE, TILE)
    return blocks.transpose(3, 1, 2, 4, 0, 5).reshape(-1, fcount, TILE)

def tiles_to_grid(tile_form, fcount):
    blocks = tile_form.reshape(N_PANEL, N_COL, CY, CX // TILE, fcount, TILE)
    return blocks.transpose(4, 1, 2, 0, 3, 5).reshape(fcount, MERIDIONAL_COUNT, ZONAL_COUNT)

def spread_tiles(flux_tiles, bank_tile_entry, conservative_overlay_factors, block_rows):
    steps_count = flux_tiles.shape[0] // block_rows

    def one_block(block_pair):
        tiles_part, offset_part = block_pair
        weights = conservative_overlay_factors[offset_part]
        return jnp.einsum('tkji,tfi->tkfj', weights, tiles_part, precision=lax.Precision.HIGHEST)
    spread = lax.map(one_block, (flux_tiles.reshape(steps_count, block_rows, 2, TILE), bank_tile_entry.reshape(steps_count, block_rows, 2)))
    return spread.reshape(-1, 2, TILE)

def gather_back(values, bank_tile_entry, conservative_overlay_factors, column_sums, block_rows):
    steps_count = values.shape[0] // block_rows

    def one_block(block_pair):
        value_part, offset_part = block_pair
        weights = conservative_overlay_factors[offset_part]
        numerator = jnp.einsum('tkji,tkfj->tfi', weights, value_part, precision=lax.Precision.HIGHEST)
        denominator = lax.optimization_barrier(jnp.sum(column_sums[offset_part], axis=1))
        return numerator / denominator[:, None, :]
    gathered = lax.map(one_block, (values.reshape(steps_count, block_rows, 2, 2, TILE), bank_tile_entry.reshape(steps_count, block_rows, 2)))
    return gathered.reshape(-1, 2, TILE)

def reference(joint_tracer_field, courant_mixing_rates, oceanic_indicator, glacial_indicator, prior_oceanic_warmth, prior_glacial_cover, partner_devices, receiving_tile_index, bank_tile_entry, conservative_overlay_factors):
    wind_east = courant_mixing_rates[0, 0, 0]
    wind_north = courant_mixing_rates[0, 1, 0]
    airflow_speed = jnp.sqrt(wind_east * wind_east + wind_north * wind_north + 0.01)
    unfrozen_share = oceanic_indicator[0].astype(jnp.float32) * (1.0 - prior_glacial_cover)
    thermal_exchange_rate = 2.0 * airflow_speed * (prior_oceanic_warmth - joint_tracer_field[0, 0, 0]) * unfrozen_share
    evaporation_rate = 2.0 * airflow_speed * (jnp.exp(0.1 * prior_oceanic_warmth) - joint_tracer_field[0, 1, 0]) * unfrozen_share
    start = joint_tracer_field.at[0, 0, 0].add(thermal_exchange_rate).at[0, 1, 0].add(evaporation_rate)
    row_open = (jnp.arange(MERIDIONAL_COUNT) < MERIDIONAL_COUNT - 1).astype(jnp.float32)[None, :, None]
    advected_list = []
    for component in range(2):
        tracer = start[component]
        east_ext = extend_grid(courant_mixing_rates[component, 0])
        north_ext = extend_grid(courant_mixing_rates[component, 1] * row_open)
        mix_ext = extend_grid(courant_mixing_rates[component, 2])
        for step_index in range(NSUB):
            tracer = advect_mix(extend_grid(tracer), east_ext, north_ext, mix_ext)
        advected_list.append(tracer)
    advected = jnp.stack(advected_list)
    surface_flux = jnp.stack([thermal_exchange_rate, evaporation_rate])
    flux_tiles = grid_to_tiles(surface_flux)
    block_rows = math.gcd(ATILES, 256)
    contrib = spread_tiles(flux_tiles, bank_tile_entry, conservative_overlay_factors, block_rows)
    targets = (partner_devices * ATILE_DEV + receiving_tile_index).reshape(-1)
    forcing_tiles = jax.ops.segment_sum(contrib, targets, num_segments=ATILES)
    forcing = tiles_to_grid(forcing_tiles, 2)
    wet = oceanic_indicator[1].astype(jnp.float32)
    new_state = advected.at[1, 0, 0].add(-(0.5 * wet * forcing[0])).at[1, 1, 0].add(0.5 * wet * forcing[1])
    sea_temp = new_state[1, 0, 0]
    ice_cover = glacial_indicator.astype(jnp.float32) * wet * jnp.clip(0.5 - sea_temp, 0.0, 1.0)
    ocean_surface = jnp.stack([sea_temp, ice_cover])
    ocean_tiles = grid_to_tiles(ocean_surface)
    values = ocean_tiles[targets].reshape(-1, 2, 2, TILE)
    column_sums = lax.optimization_barrier(jnp.sum(conservative_overlay_factors, axis=1))
    remap_back = gather_back(values, bank_tile_entry, conservative_overlay_factors, column_sums, block_rows)
    surface = jnp.stack([tiles_to_grid(remap_back, 2), ocean_surface])
    return (new_state, surface)
```

```python
import jax
import jax.numpy as jnp
from jax import lax
from jax.sharding import PartitionSpec as P

TILE = 128
NSUB = 4
HIGHEST = lax.Precision.HIGHEST


def passed_along(value, axis, steps):
    count = lax.axis_size(axis)
    initial, last = (max(0, -steps), min(count, count - steps))
    return lax.ppermute(value, axis, [(source, source + steps) for source in range(initial, last)])


def from_behind(array, axis, by):
    count = lax.axis_size(axis)
    return lax.ppermute(array, axis, [(i, (i + by) % count) for i in range(count)])


def wide_halo(array, width):
    west = from_behind(array[..., -width:], "panel", 1)
    east = from_behind(array[..., :width], "panel", -1)
    array = jnp.concatenate([west, array, east], axis=-1)
    south = passed_along(array[..., -width:, :], "col", 1)
    north = passed_along(array[..., :width, :], "col", -1)
    return jnp.concatenate([south, array, north], axis=-2)


def vertical_mix(tracer, mixing):
    level_flux = mixing[:-1] * (tracer[:, 1:] - tracer[:, :-1])
    zero_level = jnp.zeros_like(tracer[:, :1])
    from_above = jnp.concatenate([level_flux, zero_level], axis=1)
    from_below = jnp.concatenate([zero_level, level_flux], axis=1)
    relaxation = jnp.concatenate(
        [jnp.zeros_like(tracer[:, :-1]), mixing[-1:] * tracer[:, -1:]], axis=1
    )
    return tracer + from_above - from_below - relaxation


def advect_mix(tracer, east_vel, north_vel, mixing):
    centre = tracer[..., 1:-1, 1:-1]
    vel_east = east_vel[:, 1:-1, 1:-1]
    vel_west = east_vel[:, 1:-1, :-2]
    vel_north = north_vel[:, 1:-1, 1:-1]
    vel_south = north_vel[:, :-2, 1:-1]
    flux_east = (
        jnp.maximum(vel_east, 0.0) * centre + jnp.minimum(vel_east, 0.0) * tracer[..., 1:-1, 2:]
    )
    flux_west = (
        jnp.maximum(vel_west, 0.0) * tracer[..., 1:-1, :-2] + jnp.minimum(vel_west, 0.0) * centre
    )
    flux_north = (
        jnp.maximum(vel_north, 0.0) * centre + jnp.minimum(vel_north, 0.0) * tracer[..., 2:, 1:-1]
    )
    flux_south = (
        jnp.maximum(vel_south, 0.0) * tracer[..., :-2, 1:-1] + jnp.minimum(vel_south, 0.0) * centre
    )
    advanced = centre - (flux_east - flux_west) - (flux_north - flux_south)
    return vertical_mix(advanced, mixing[:, 1:-1, 1:-1])


def to_tiles(field_grid):
    fcount, grid_rows, grid_cols = field_grid.shape
    blocks = field_grid.reshape(fcount, grid_rows, grid_cols // TILE, TILE)
    return blocks.transpose(1, 2, 0, 3).reshape(-1, fcount, TILE)


def from_tiles(tile_form, grid_rows, grid_cols):
    fcount = tile_form.shape[1]
    blocks = tile_form.reshape(grid_rows, grid_cols // TILE, fcount, TILE)
    return blocks.transpose(2, 0, 1, 3).reshape(fcount, grid_rows, grid_cols)


def bucket_places(partner_devices, owners, capacity):
    owner_list = partner_devices.reshape(-1)
    owner_hit = (owner_list[:, None] == jnp.arange(owners, dtype=jnp.int32)[None, :]).astype(
        jnp.int32
    )
    owner_rank = jnp.cumsum(owner_hit, axis=0) - owner_hit
    position = jnp.sum(owner_rank * owner_hit, axis=1)
    return owner_list * capacity + position


def advect(start, coeffs, grid_rows):
    fields = start.shape[0] * start.shape[1]
    both = jnp.concatenate([start.reshape((fields,) + start.shape[2:]), coeffs.reshape((-1,) + coeffs.shape[2:])])
    wide = wide_halo(both, NSUB)
    levels = coeffs.shape[1]
    tracer = wide[:fields].reshape(start.shape[:2] + wide.shape[1:])
    coeff_ext = wide[fields:].reshape((3, levels) + wide.shape[1:])
    rows_total = grid_rows * lax.axis_size("col")
    row_global = (
        lax.axis_index("col") * grid_rows
        + jnp.arange(grid_rows + 2 * NSUB, dtype=jnp.int32)
        - NSUB
    )
    row_open = ((row_global >= 0) & (row_global < rows_total - 1)).astype(jnp.float32)
    east_ext = coeff_ext[0]
    north_ext = coeff_ext[1] * row_open[None, :, None]
    mix_ext = coeff_ext[2]
    for step_index in range(NSUB):
        s = step_index
        e = east_ext.shape[1] - s
        w = east_ext.shape[2] - s
        tracer = advect_mix(
            tracer,
            east_ext[:, s:e, s:w],
            north_ext[:, s:e, s:w],
            mix_ext[:, s:e, s:w],
        )
    return tracer


def on_device(
    joint_tracer_field,
    courant_mixing_rates,
    oceanic_indicator,
    glacial_indicator,
    prior_oceanic_warmth,
    prior_glacial_cover,
    partner_devices,
    receiving_tile_index,
    bank_tile_entry,
    conservative_overlay_factors,
):
    owners = lax.axis_size("panel") * lax.axis_size("col")
    tile_count = partner_devices.shape[0]
    capacity = max(2, 4 * tile_count // owners)
    slots = owners * capacity
    nbank = conservative_overlay_factors.shape[0]
    on_atmos = lax.axis_index("comp") == 0
    device_tracer_share = joint_tracer_field[0]
    coeffs = courant_mixing_rates[0]
    grid_rows = coeffs.shape[2]
    grid_cols = coeffs.shape[3]
    sea_here = oceanic_indicator[0].astype(jnp.float32)
    wind_east = coeffs[0, 0]
    wind_north = coeffs[1, 0]
    airflow_speed = jnp.sqrt(wind_east * wind_east + wind_north * wind_north + 0.01)
    unfrozen_share = sea_here * (1.0 - prior_glacial_cover)
    thermal_exchange_rate = (
        2.0 * airflow_speed * (prior_oceanic_warmth - device_tracer_share[0, 0]) * unfrozen_share
    )
    evaporation_rate = (
        2.0
        * airflow_speed
        * (jnp.exp(0.1 * prior_oceanic_warmth) - device_tracer_share[1, 0])
        * unfrozen_share
    )
    heated = device_tracer_share.at[0, 0].add(thermal_exchange_rate).at[1, 0].add(evaporation_rate)
    start = jnp.where(on_atmos, heated, device_tracer_share)
    surface_flux = jnp.stack([thermal_exchange_rate, evaporation_rate])
    flux_tiles = passed_along(to_tiles(surface_flux), "comp", 1)

    flux_rows = flux_tiles.reshape(tile_count * 2, TILE)
    by_bank = jnp.einsum(
        "bji,ri->brj", conservative_overlay_factors, flux_rows, precision=HIGHEST
    ).reshape(nbank * tile_count, 2 * TILE)
    tile_ids = jnp.arange(tile_count, dtype=jnp.int32)[:, None]
    pair_rows = bank_tile_entry * tile_count + tile_ids
    contrib = by_bank[pair_rows.reshape(-1)]

    bucket_place = bucket_places(partner_devices, owners, capacity)
    slot_list = receiving_tile_index.reshape(-1)
    place_match = bucket_place[None, :] == jnp.arange(slots, dtype=jnp.int32)[:, None]
    place_hit = place_match.astype(jnp.float32)
    buffer = jnp.dot(place_hit, contrib, precision=HIGHEST).reshape(owners, capacity, 2, TILE)
    labels = jnp.sum(jnp.where(place_match, slot_list[None, :], 0), axis=1).reshape(
        owners, capacity
    )
    received = lax.all_to_all(buffer, ("panel", "col"), 0, 0, tiled=True)
    recv_slots = lax.all_to_all(labels, ("panel", "col"), 0, 0, tiled=True)
    slot_hit = (
        recv_slots.reshape(-1)[None, :] == jnp.arange(tile_count, dtype=jnp.int32)[:, None]
    ).astype(jnp.float32)
    summed = jnp.dot(slot_hit, received.reshape(slots, 2 * TILE), precision=HIGHEST)
    forcing = from_tiles(summed.reshape(tile_count, 2, TILE), grid_rows, grid_cols)

    tracer = advect(start, coeffs, grid_rows)
    forced = (
        tracer.at[0, 0]
        .add(-(0.5 * sea_here * forcing[0]))
        .at[1, 0]
        .add(0.5 * sea_here * forcing[1])
    )
    new_here = jnp.where(on_atmos, tracer, forced)
    sea_temp = new_here[0, 0]
    ice_cover = (
        glacial_indicator.astype(jnp.float32) * sea_here * jnp.clip(0.5 - sea_temp, 0.0, 1.0)
    )
    ocean_surface = jnp.stack([sea_temp, ice_cover])
    ocean_tiles = to_tiles(ocean_surface).reshape(tile_count, 2 * TILE)
    reply = jnp.einsum("ts,tc->sc", slot_hit, ocean_tiles, precision=HIGHEST)
    returned = lax.all_to_all(
        reply.reshape(owners, capacity, 2 * TILE), ("panel", "col"), 0, 0, tiled=True
    ).reshape(slots, 2 * TILE)
    values = jnp.einsum("sp,sc->pc", place_hit, returned, precision=HIGHEST)

    by_bank_back = jnp.einsum(
        "rj,bji->bri",
        values.reshape(tile_count * 4, TILE),
        conservative_overlay_factors,
        precision=HIGHEST,
    ).reshape(nbank * tile_count, 4 * TILE)
    first = by_bank_back[pair_rows[:, 0]][:, : 2 * TILE]
    second = by_bank_back[pair_rows[:, 1]][:, 2 * TILE :]
    column_sums = jnp.sum(conservative_overlay_factors, axis=1)
    denominator = column_sums[bank_tile_entry[:, 0]] + column_sums[bank_tile_entry[:, 1]]
    remap_back = (first + second).reshape(tile_count, 2, TILE) / denominator[:, None, :]
    remapped = passed_along(from_tiles(remap_back, grid_rows, grid_cols), "comp", -1)
    surface_here = jnp.where(on_atmos, remapped, ocean_surface)
    return (new_here[None], surface_here[None])


def solution(mesh):
    return jax.shard_map(
        on_device,
        mesh=mesh,
        in_specs=(
            P("comp", None, None, "col", "panel"),
            P("comp", None, None, "col", "panel"),
            P("comp", "col", "panel"),
            P("col", "panel"),
            P("col", "panel"),
            P("col", "panel"),
            P(("panel", "col"), None),
            P(("panel", "col"), None),
            P(("panel", "col"), None),
            P(),
        ),
        out_specs=(P("comp", None, None, "col", "panel"), P("comp", None, "col", "panel")),
        check_vma=False,
    )
```

```python
import jax
import jax.numpy as jnp
from jax import lax
from jax.sharding import PartitionSpec as P

TILE = 128
NSUB = 4
HIGHEST = lax.Precision.HIGHEST


def passed_along(value, axis, steps):
    count = lax.axis_size(axis)
    initial, last = (max(0, -steps), min(count, count - steps))
    return lax.ppermute(value, axis, [(source, source + steps) for source in range(initial, last)])


def from_behind(array, axis, by):
    count = lax.axis_size(axis)
    return lax.ppermute(array, axis, [(i, (i + by) % count) for i in range(count)])


def wide_halo(array, width):
    west = from_behind(array[..., -width:], "panel", 1)
    east = from_behind(array[..., :width], "panel", -1)
    array = jnp.concatenate([west, array, east], axis=-1)
    south = passed_along(array[..., -width:, :], "col", 1)
    north = passed_along(array[..., :width, :], "col", -1)
    return jnp.concatenate([south, array, north], axis=-2)


def vertical_mix(tracer, mixing):
    level_flux = mixing[:-1] * (tracer[:, 1:] - tracer[:, :-1])
    zero_level = jnp.zeros_like(tracer[:, :1])
    from_above = jnp.concatenate([level_flux, zero_level], axis=1)
    from_below = jnp.concatenate([zero_level, level_flux], axis=1)
    relaxation = jnp.concatenate(
        [jnp.zeros_like(tracer[:, :-1]), mixing[-1:] * tracer[:, -1:]], axis=1
    )
    return tracer + from_above - from_below - relaxation


def advect_mix(tracer, east_vel, north_vel, mixing):
    centre = tracer[..., 1:-1, 1:-1]
    vel_east = east_vel[:, 1:-1, 1:-1]
    vel_west = east_vel[:, 1:-1, :-2]
    vel_north = north_vel[:, 1:-1, 1:-1]
    vel_south = north_vel[:, :-2, 1:-1]
    flux_east = (
        jnp.maximum(vel_east, 0.0) * centre + jnp.minimum(vel_east, 0.0) * tracer[..., 1:-1, 2:]
    )
    flux_west = (
        jnp.maximum(vel_west, 0.0) * tracer[..., 1:-1, :-2] + jnp.minimum(vel_west, 0.0) * centre
    )
    flux_north = (
        jnp.maximum(vel_north, 0.0) * centre + jnp.minimum(vel_north, 0.0) * tracer[..., 2:, 1:-1]
    )
    flux_south = (
        jnp.maximum(vel_south, 0.0) * tracer[..., :-2, 1:-1] + jnp.minimum(vel_south, 0.0) * centre
    )
    advanced = centre - (flux_east - flux_west) - (flux_north - flux_south)
    return vertical_mix(advanced, mixing[:, 1:-1, 1:-1])


def to_tiles(field_grid):
    fcount, grid_rows, grid_cols = field_grid.shape
    blocks = field_grid.reshape(fcount, grid_rows, grid_cols // TILE, TILE)
    return blocks.transpose(1, 2, 0, 3).reshape(-1, fcount, TILE)


def from_tiles(tile_form, grid_rows, grid_cols):
    fcount = tile_form.shape[1]
    blocks = tile_form.reshape(grid_rows, grid_cols // TILE, fcount, TILE)
    return blocks.transpose(2, 0, 1, 3).reshape(fcount, grid_rows, grid_cols)


def bucket_places(partner_devices, owners, capacity):
    owner_list = partner_devices.reshape(-1)
    owner_hit = (owner_list[:, None] == jnp.arange(owners, dtype=jnp.int32)[None, :]).astype(
        jnp.int32
    )
    owner_rank = jnp.cumsum(owner_hit, axis=0) - owner_hit
    position = jnp.sum(owner_rank * owner_hit, axis=1)
    return owner_list * capacity + position


def advect(start, coeffs, grid_rows):
    fields = start.shape[0] * start.shape[1]
    both = jnp.concatenate([start.reshape((fields,) + start.shape[2:]), coeffs.reshape((-1,) + coeffs.shape[2:])])
    wide = wide_halo(both, NSUB)
    levels = coeffs.shape[1]
    tracer = wide[:fields].reshape(start.shape[:2] + wide.shape[1:])
    coeff_ext = wide[fields:].reshape((3, levels) + wide.shape[1:])
    rows_total = grid_rows * lax.axis_size("col")
    row_global = (
        lax.axis_index("col") * grid_rows
        + jnp.arange(grid_rows + 2 * NSUB, dtype=jnp.int32)
        - NSUB
    )
    row_open = ((row_global >= 0) & (row_global < rows_total - 1)).astype(jnp.float32)
    east_ext = coeff_ext[0]
    north_ext = coeff_ext[1] * row_open[None, :, None]
    mix_ext = coeff_ext[2]
    for step_index in range(NSUB):
        s = step_index
        e = east_ext.shape[1] - s
        w = east_ext.shape[2] - s
        tracer = advect_mix(
            tracer,
            east_ext[:, s:e, s:w],
            north_ext[:, s:e, s:w],
            mix_ext[:, s:e, s:w],
        )
    return tracer


def on_device(
    joint_tracer_field,
    courant_mixing_rates,
    oceanic_indicator,
    glacial_indicator,
    prior_oceanic_warmth,
    prior_glacial_cover,
    partner_devices,
    receiving_tile_index,
    bank_tile_entry,
    conservative_overlay_factors,
):
    owners = lax.axis_size("panel") * lax.axis_size("col")
    tile_count = partner_devices.shape[0]
    capacity = max(2, 4 * tile_count // owners)
    slots = owners * capacity
    nbank = conservative_overlay_factors.shape[0]
    on_atmos = lax.axis_index("comp") == 0
    device_tracer_share = joint_tracer_field[0]
    coeffs = courant_mixing_rates[0]
    grid_rows = coeffs.shape[2]
    grid_cols = coeffs.shape[3]
    sea_here = oceanic_indicator[0].astype(jnp.float32)
    wind_east = coeffs[0, 0]
    wind_north = coeffs[1, 0]
    airflow_speed = jnp.sqrt(wind_east * wind_east + wind_north * wind_north + 0.01)
    unfrozen_share = sea_here * (1.0 - prior_glacial_cover)
    thermal_exchange_rate = (
        2.0 * airflow_speed * (prior_oceanic_warmth - device_tracer_share[0, 0]) * unfrozen_share
    )
    evaporation_rate = (
        2.0
        * airflow_speed
        * (jnp.exp(0.1 * prior_oceanic_warmth) - device_tracer_share[1, 0])
        * unfrozen_share
    )
    heated = device_tracer_share.at[0, 0].add(thermal_exchange_rate).at[1, 0].add(evaporation_rate)
    start = jnp.where(on_atmos, heated, device_tracer_share)
    surface_flux = jnp.stack([thermal_exchange_rate, evaporation_rate])
    flux_rows = passed_along(to_tiles(surface_flux), "comp", 1).reshape(tile_count * 2, TILE)
    pairs = tile_count * 2
    me = lax.axis_index("panel") * lax.axis_size("col") + lax.axis_index("col")

    bucket_place = bucket_places(partner_devices, owners, capacity)
    place_match = bucket_place[None, :] == jnp.arange(slots, dtype=jnp.int32)[:, None]
    slot_used = jnp.any(place_match, axis=1)
    slot_pair = jnp.sum(jnp.where(place_match, jnp.arange(pairs, dtype=jnp.int32)[None, :], 0), axis=1)
    slot_tile = slot_pair // 2
    slot_bank = bank_tile_entry.reshape(-1)[slot_pair]

    by_bank = jnp.einsum(
        "bji,ri->brj", conservative_overlay_factors, flux_rows, precision=HIGHEST
    ).reshape(nbank * pairs, TILE)
    f_ids = jnp.arange(2, dtype=jnp.int32)[None, :]
    slot_rows = (slot_bank * pairs + slot_tile * 2)[:, None] + f_ids
    picked = by_bank[slot_rows.reshape(-1)].reshape(slots, 2, TILE)
    buffer = jnp.where(slot_used[:, None, None], picked, 0.0).reshape(owners, capacity * 2, TILE)
    received = lax.all_to_all(buffer, ("panel", "col"), 0, 0, tiled=True).reshape(slots * 2, TILE)

    routes = lax.all_gather(
        jnp.concatenate([partner_devices.T, receiving_tile_index.T], axis=0), ("panel", "col")
    )
    mine = [(routes[:, k] == me).astype(jnp.int32) for k in range(2)]
    per_tile = mine[0] + mine[1]
    before = jnp.cumsum(per_tile, axis=1) - per_tile
    rank = [before, before + mine[0]]
    recv_slots = jnp.stack(
        [
            sum(jnp.sum(mine[k] * (rank[k] == c) * routes[:, 2 + k], axis=1) for k in range(2))
            for c in range(capacity)
        ],
        axis=1,
    ).reshape(-1)
    row_ids = lax.broadcasted_iota(jnp.int32, (pairs, slots * 2), 0)
    col_ids = lax.broadcasted_iota(jnp.int32, (pairs, slots * 2), 1)
    recv_rep = jnp.broadcast_to(recv_slots[:, None], (slots, 2)).reshape(-1)
    slot_hit2 = (
        (recv_rep[None, :] == row_ids // 2) & (col_ids % 2 == row_ids % 2)
    ).astype(jnp.float32)
    summed = jnp.dot(slot_hit2, received, precision=HIGHEST)
    forcing = from_tiles(summed.reshape(tile_count, 2, TILE), grid_rows, grid_cols)

    tracer = advect(start, coeffs, grid_rows)
    forced = (
        tracer.at[0, 0]
        .add(-(0.5 * sea_here * forcing[0]))
        .at[1, 0]
        .add(0.5 * sea_here * forcing[1])
    )
    new_here = jnp.where(on_atmos, tracer, forced)
    sea_temp = new_here[0, 0]
    ice_cover = (
        glacial_indicator.astype(jnp.float32) * sea_here * jnp.clip(0.5 - sea_temp, 0.0, 1.0)
    )
    ocean_surface = jnp.stack([sea_temp, ice_cover])
    ocean_tiles = to_tiles(ocean_surface).reshape(pairs, TILE)
    reply = jnp.dot(slot_hit2.T, ocean_tiles, precision=HIGHEST).reshape(owners, capacity * 2, TILE)
    returned = lax.all_to_all(reply, ("panel", "col"), 0, 0, tiled=True).reshape(slots * 2, TILE)
    place_rep = jnp.broadcast_to(bucket_place[:, None], (pairs, 2)).reshape(-1)
    p_rows = lax.broadcasted_iota(jnp.int32, (pairs * 2, slots * 2), 0)
    p_cols = lax.broadcasted_iota(jnp.int32, (pairs * 2, slots * 2), 1)
    place_hit2 = ((place_rep[:, None] == p_cols // 2) & (p_cols % 2 == p_rows % 2)).astype(
        jnp.float32
    )
    values = jnp.dot(place_hit2, returned, precision=HIGHEST)

    by_bank_back = jnp.einsum(
        "rj,bji->bri", values, conservative_overlay_factors, precision=HIGHEST
    ).reshape(nbank * pairs * 2, TILE)
    tile_ids = jnp.arange(tile_count, dtype=jnp.int32)[:, None]
    pair_rows = (bank_tile_entry * tile_count + tile_ids) * 4 + jnp.arange(2, dtype=jnp.int32)[None, :] * 2
    back_rows = pair_rows[:, :, None] + f_ids[:, None, :]
    numerator = jnp.sum(by_bank_back[back_rows.reshape(-1)].reshape(tile_count, 2, 2, TILE), axis=1)
    column_sums = jnp.sum(conservative_overlay_factors, axis=1)
    denominator = column_sums[bank_tile_entry[:, 0]] + column_sums[bank_tile_entry[:, 1]]
    remap_back = numerator / denominator[:, None, :]
    remapped = passed_along(from_tiles(remap_back, grid_rows, grid_cols), "comp", -1)
    surface_here = jnp.where(on_atmos, remapped, ocean_surface)
    return (new_here[None], surface_here[None])


def solution(mesh):
    return jax.shard_map(
        on_device,
        mesh=mesh,
        in_specs=(
            P("comp", None, None, "col", "panel"),
            P("comp", None, None, "col", "panel"),
            P("comp", "col", "panel"),
            P("col", "panel"),
            P("col", "panel"),
            P("col", "panel"),
            P(("panel", "col"), None),
            P(("panel", "col"), None),
            P(("panel", "col"), None),
            P(),
        ),
        out_specs=(P("comp", None, None, "col", "panel"), P("comp", None, "col", "panel")),
        check_vma=False,
    )
```

```python
import jax
import jax.numpy as jnp
from jax import lax
from jax.sharding import PartitionSpec as P

TILE = 128
NSUB = 4
HIGHEST = lax.Precision.HIGHEST


def passed_along(value, axis, steps):
    count = lax.axis_size(axis)
    initial, last = (max(0, -steps), min(count, count - steps))
    return lax.ppermute(value, axis, [(source, source + steps) for source in range(initial, last)])


def from_behind(array, axis, by):
    count = lax.axis_size(axis)
    return lax.ppermute(array, axis, [(i, (i + by) % count) for i in range(count)])


def wide_halo(array, width):
    west = from_behind(array[..., -width:], "panel", 1)
    east = from_behind(array[..., :width], "panel", -1)
    array = jnp.concatenate([west, array, east], axis=-1)
    south = passed_along(array[..., -width:, :], "col", 1)
    north = passed_along(array[..., :width, :], "col", -1)
    return jnp.concatenate([south, array, north], axis=-2)


def vertical_mix(tracer, mixing):
    level_flux = mixing[:-1] * (tracer[:, 1:] - tracer[:, :-1])
    zero_level = jnp.zeros_like(tracer[:, :1])
    from_above = jnp.concatenate([level_flux, zero_level], axis=1)
    from_below = jnp.concatenate([zero_level, level_flux], axis=1)
    relaxation = jnp.concatenate(
        [jnp.zeros_like(tracer[:, :-1]), mixing[-1:] * tracer[:, -1:]], axis=1
    )
    return tracer + from_above - from_below - relaxation


def advect_mix(tracer, east_vel, north_vel, mixing):
    centre = tracer[..., 1:-1, 1:-1]
    vel_east = east_vel[:, 1:-1, 1:-1]
    vel_west = east_vel[:, 1:-1, :-2]
    vel_north = north_vel[:, 1:-1, 1:-1]
    vel_south = north_vel[:, :-2, 1:-1]
    flux_east = (
        jnp.maximum(vel_east, 0.0) * centre + jnp.minimum(vel_east, 0.0) * tracer[..., 1:-1, 2:]
    )
    flux_west = (
        jnp.maximum(vel_west, 0.0) * tracer[..., 1:-1, :-2] + jnp.minimum(vel_west, 0.0) * centre
    )
    flux_north = (
        jnp.maximum(vel_north, 0.0) * centre + jnp.minimum(vel_north, 0.0) * tracer[..., 2:, 1:-1]
    )
    flux_south = (
        jnp.maximum(vel_south, 0.0) * tracer[..., :-2, 1:-1] + jnp.minimum(vel_south, 0.0) * centre
    )
    advanced = centre - (flux_east - flux_west) - (flux_north - flux_south)
    return vertical_mix(advanced, mixing[:, 1:-1, 1:-1])


def to_tiles(field_grid):
    fcount, grid_rows, grid_cols = field_grid.shape
    blocks = field_grid.reshape(fcount, grid_rows, grid_cols // TILE, TILE)
    return blocks.transpose(1, 2, 0, 3).reshape(-1, fcount, TILE)


def from_tiles(tile_form, grid_rows, grid_cols):
    fcount = tile_form.shape[1]
    blocks = tile_form.reshape(grid_rows, grid_cols // TILE, fcount, TILE)
    return blocks.transpose(2, 0, 1, 3).reshape(fcount, grid_rows, grid_cols)


def bucket_places(partner_devices, owners, capacity):
    owner_list = partner_devices.reshape(-1)
    owner_hit = (owner_list[:, None] == jnp.arange(owners, dtype=jnp.int32)[None, :]).astype(
        jnp.int32
    )
    owner_rank = jnp.cumsum(owner_hit, axis=0) - owner_hit
    position = jnp.sum(owner_rank * owner_hit, axis=1)
    return owner_list * capacity + position


def advect(start, coeffs, grid_rows):
    fields = start.shape[0] * start.shape[1]
    both = jnp.concatenate([start.reshape((fields,) + start.shape[2:]), coeffs.reshape((-1,) + coeffs.shape[2:])])
    wide = wide_halo(both, NSUB)
    levels = coeffs.shape[1]
    tracer = wide[:fields].reshape(start.shape[:2] + wide.shape[1:])
    coeff_ext = wide[fields:].reshape((3, levels) + wide.shape[1:])
    rows_total = grid_rows * lax.axis_size("col")
    row_global = (
        lax.axis_index("col") * grid_rows
        + jnp.arange(grid_rows + 2 * NSUB, dtype=jnp.int32)
        - NSUB
    )
    row_open = ((row_global >= 0) & (row_global < rows_total - 1)).astype(jnp.float32)
    east_ext = coeff_ext[0]
    north_ext = coeff_ext[1] * row_open[None, :, None]
    mix_ext = coeff_ext[2]
    for step_index in range(NSUB):
        s = step_index
        e = east_ext.shape[1] - s
        w = east_ext.shape[2] - s
        tracer = advect_mix(
            tracer,
            east_ext[:, s:e, s:w],
            north_ext[:, s:e, s:w],
            mix_ext[:, s:e, s:w],
        )
    return tracer


def on_device(
    joint_tracer_field,
    courant_mixing_rates,
    oceanic_indicator,
    glacial_indicator,
    prior_oceanic_warmth,
    prior_glacial_cover,
    partner_devices,
    receiving_tile_index,
    bank_tile_entry,
    conservative_overlay_factors,
):
    owners = lax.axis_size("panel") * lax.axis_size("col")
    tile_count = partner_devices.shape[0]
    capacity = max(2, 4 * tile_count // owners)
    slots = owners * capacity
    nbank = conservative_overlay_factors.shape[0]
    on_atmos = lax.axis_index("comp") == 0
    device_tracer_share = joint_tracer_field[0]
    coeffs = courant_mixing_rates[0]
    grid_rows = coeffs.shape[2]
    grid_cols = coeffs.shape[3]
    sea_here = oceanic_indicator[0].astype(jnp.float32)
    wind_east = coeffs[0, 0]
    wind_north = coeffs[1, 0]
    airflow_speed = jnp.sqrt(wind_east * wind_east + wind_north * wind_north + 0.01)
    unfrozen_share = sea_here * (1.0 - prior_glacial_cover)
    thermal_exchange_rate = (
        2.0 * airflow_speed * (prior_oceanic_warmth - device_tracer_share[0, 0]) * unfrozen_share
    )
    evaporation_rate = (
        2.0
        * airflow_speed
        * (jnp.exp(0.1 * prior_oceanic_warmth) - device_tracer_share[1, 0])
        * unfrozen_share
    )
    heated = device_tracer_share.at[0, 0].add(thermal_exchange_rate).at[1, 0].add(evaporation_rate)
    start = jnp.where(on_atmos, heated, device_tracer_share)
    surface_flux = jnp.stack([thermal_exchange_rate, evaporation_rate])
    flux_rows = passed_along(to_tiles(surface_flux), "comp", 1).reshape(tile_count * 2, TILE)
    pairs = tile_count * 2

    bucket_place = bucket_places(partner_devices, owners, capacity)
    place_match = bucket_place[None, :] == jnp.arange(slots, dtype=jnp.int32)[:, None]
    slot_used = jnp.any(place_match, axis=1)
    slot_pair = jnp.sum(jnp.where(place_match, jnp.arange(pairs, dtype=jnp.int32)[None, :], 0), axis=1)
    slot_tile = slot_pair // 2
    slot_bank = bank_tile_entry.reshape(-1)[slot_pair]

    by_bank = jnp.einsum(
        "bji,ri->brj", conservative_overlay_factors, flux_rows, precision=HIGHEST
    ).reshape(nbank * pairs, TILE)
    f_ids = jnp.arange(2, dtype=jnp.int32)[None, :]
    slot_rows = (slot_bank * pairs + slot_tile * 2)[:, None] + f_ids
    picked = by_bank[slot_rows.reshape(-1)].reshape(slots, 2, TILE)
    buffer = jnp.where(slot_used[:, None, None], picked, 0.0).reshape(owners, capacity * 2, TILE)
    slot_label = jnp.where(slot_used, receiving_tile_index.reshape(-1)[slot_pair], 0)
    label_row = jnp.pad(
        slot_label.reshape(owners, capacity).astype(jnp.float32), ((0, 0), (0, TILE - capacity))
    )
    bucket = jnp.concatenate([buffer, label_row[:, None, :]], axis=1)
    arrived = lax.all_to_all(bucket, ("panel", "col"), 0, 0, tiled=True)
    received = arrived[:, : capacity * 2].reshape(slots * 2, TILE)
    recv_slots = arrived[:, capacity * 2, :capacity].astype(jnp.int32).reshape(-1)

    row_ids = lax.broadcasted_iota(jnp.int32, (pairs, slots * 2), 0)
    col_ids = lax.broadcasted_iota(jnp.int32, (pairs, slots * 2), 1)
    recv_rep = jnp.broadcast_to(recv_slots[:, None], (slots, 2)).reshape(-1)
    slot_hit2 = (
        (recv_rep[None, :] == row_ids // 2) & (col_ids % 2 == row_ids % 2)
    ).astype(jnp.float32)
    summed = jnp.dot(slot_hit2, received, precision=HIGHEST)
    forcing = from_tiles(summed.reshape(tile_count, 2, TILE), grid_rows, grid_cols)

    tracer = advect(start, coeffs, grid_rows)
    forced = (
        tracer.at[0, 0]
        .add(-(0.5 * sea_here * forcing[0]))
        .at[1, 0]
        .add(0.5 * sea_here * forcing[1])
    )
    new_here = jnp.where(on_atmos, tracer, forced)
    sea_temp = new_here[0, 0]
    ice_cover = (
        glacial_indicator.astype(jnp.float32) * sea_here * jnp.clip(0.5 - sea_temp, 0.0, 1.0)
    )
    ocean_surface = jnp.stack([sea_temp, ice_cover])
    ocean_tiles = to_tiles(ocean_surface).reshape(pairs, TILE)
    reply = jnp.dot(slot_hit2.T, ocean_tiles, precision=HIGHEST).reshape(owners, capacity * 2, TILE)
    returned = lax.all_to_all(reply, ("panel", "col"), 0, 0, tiled=True).reshape(slots * 2, TILE)
    place_rep = jnp.broadcast_to(bucket_place[:, None], (pairs, 2)).reshape(-1)
    p_rows = lax.broadcasted_iota(jnp.int32, (pairs * 2, slots * 2), 0)
    p_cols = lax.broadcasted_iota(jnp.int32, (pairs * 2, slots * 2), 1)
    place_hit2 = ((place_rep[:, None] == p_cols // 2) & (p_cols % 2 == p_rows % 2)).astype(
        jnp.float32
    )
    values = jnp.dot(place_hit2, returned, precision=HIGHEST)

    by_bank_back = jnp.einsum(
        "rj,bji->bri", values, conservative_overlay_factors, precision=HIGHEST
    ).reshape(nbank * pairs * 2, TILE)
    tile_ids = jnp.arange(tile_count, dtype=jnp.int32)[:, None]
    pair_rows = (bank_tile_entry * tile_count + tile_ids) * 4 + jnp.arange(2, dtype=jnp.int32)[None, :] * 2
    back_rows = pair_rows[:, :, None] + f_ids[:, None, :]
    numerator = jnp.sum(by_bank_back[back_rows.reshape(-1)].reshape(tile_count, 2, 2, TILE), axis=1)
    column_sums = jnp.sum(conservative_overlay_factors, axis=1)
    denominator = column_sums[bank_tile_entry[:, 0]] + column_sums[bank_tile_entry[:, 1]]
    remap_back = numerator / denominator[:, None, :]
    remapped = passed_along(from_tiles(remap_back, grid_rows, grid_cols), "comp", -1)
    surface_here = jnp.where(on_atmos, remapped, ocean_surface)
    return (new_here[None], surface_here[None])


def solution(mesh):
    return jax.shard_map(
        on_device,
        mesh=mesh,
        in_specs=(
            P("comp", None, None, "col", "panel"),
            P("comp", None, None, "col", "panel"),
            P("comp", "col", "panel"),
            P("col", "panel"),
            P("col", "panel"),
            P("col", "panel"),
            P(("panel", "col"), None),
            P(("panel", "col"), None),
            P(("panel", "col"), None),
            P(),
        ),
        out_specs=(P("comp", None, None, "col", "panel"), P("comp", None, "col", "panel")),
        check_vma=False,
    )
```

```python
import jax
import jax.numpy as jnp
from jax import lax
from jax.sharding import PartitionSpec as P

TILE = 128
NSUB = 4
HIGHEST = lax.Precision.HIGHEST


def passed_along(value, axis, steps):
    count = lax.axis_size(axis)
    initial, last = (max(0, -steps), min(count, count - steps))
    return lax.ppermute(value, axis, [(source, source + steps) for source in range(initial, last)])


def from_behind(array, axis, by):
    count = lax.axis_size(axis)
    return lax.ppermute(array, axis, [(i, (i + by) % count) for i in range(count)])


def wide_halo(array, width):
    west = from_behind(array[..., -width:], "panel", 1)
    east = from_behind(array[..., :width], "panel", -1)
    array = jnp.concatenate([west, array, east], axis=-1)
    south = passed_along(array[..., -width:, :], "col", 1)
    north = passed_along(array[..., :width, :], "col", -1)
    return jnp.concatenate([south, array, north], axis=-2)


def vertical_mix(tracer, mixing):
    level_flux = mixing[:-1] * (tracer[:, 1:] - tracer[:, :-1])
    zero_level = jnp.zeros_like(tracer[:, :1])
    from_above = jnp.concatenate([level_flux, zero_level], axis=1)
    from_below = jnp.concatenate([zero_level, level_flux], axis=1)
    relaxation = jnp.concatenate(
        [jnp.zeros_like(tracer[:, :-1]), mixing[-1:] * tracer[:, -1:]], axis=1
    )
    return tracer + from_above - from_below - relaxation


def advect_mix(tracer, east_vel, north_vel, mixing):
    centre = tracer[..., 1:-1, 1:-1]
    vel_east = east_vel[:, 1:-1, 1:-1]
    vel_west = east_vel[:, 1:-1, :-2]
    vel_north = north_vel[:, 1:-1, 1:-1]
    vel_south = north_vel[:, :-2, 1:-1]
    flux_east = (
        jnp.maximum(vel_east, 0.0) * centre + jnp.minimum(vel_east, 0.0) * tracer[..., 1:-1, 2:]
    )
    flux_west = (
        jnp.maximum(vel_west, 0.0) * tracer[..., 1:-1, :-2] + jnp.minimum(vel_west, 0.0) * centre
    )
    flux_north = (
        jnp.maximum(vel_north, 0.0) * centre + jnp.minimum(vel_north, 0.0) * tracer[..., 2:, 1:-1]
    )
    flux_south = (
        jnp.maximum(vel_south, 0.0) * tracer[..., :-2, 1:-1] + jnp.minimum(vel_south, 0.0) * centre
    )
    advanced = centre - (flux_east - flux_west) - (flux_north - flux_south)
    return vertical_mix(advanced, mixing[:, 1:-1, 1:-1])


def to_tiles(field_grid):
    fcount, grid_rows, grid_cols = field_grid.shape
    blocks = field_grid.reshape(fcount, grid_rows, grid_cols // TILE, TILE)
    return blocks.transpose(1, 2, 0, 3).reshape(-1, fcount, TILE)


def from_tiles(tile_form, grid_rows, grid_cols):
    fcount = tile_form.shape[1]
    blocks = tile_form.reshape(grid_rows, grid_cols // TILE, fcount, TILE)
    return blocks.transpose(2, 0, 1, 3).reshape(fcount, grid_rows, grid_cols)


def bucket_places(partner_devices, owners, capacity):
    owner_list = partner_devices.reshape(-1)
    owner_hit = (owner_list[:, None] == jnp.arange(owners, dtype=jnp.int32)[None, :]).astype(
        jnp.int32
    )
    owner_rank = jnp.cumsum(owner_hit, axis=0) - owner_hit
    position = jnp.sum(owner_rank * owner_hit, axis=1)
    return owner_list * capacity + position


def advect(start, coeffs, grid_rows):
    fields = start.shape[0] * start.shape[1]
    both = jnp.concatenate([start.reshape((fields,) + start.shape[2:]), coeffs.reshape((-1,) + coeffs.shape[2:])])
    wide = wide_halo(both, NSUB)
    levels = coeffs.shape[1]
    tracer = wide[:fields].reshape(start.shape[:2] + wide.shape[1:])
    coeff_ext = wide[fields:].reshape((3, levels) + wide.shape[1:])
    rows_total = grid_rows * lax.axis_size("col")
    row_global = (
        lax.axis_index("col") * grid_rows
        + jnp.arange(grid_rows + 2 * NSUB, dtype=jnp.int32)
        - NSUB
    )
    row_open = ((row_global >= 0) & (row_global < rows_total - 1)).astype(jnp.float32)
    east_ext = coeff_ext[0]
    north_ext = coeff_ext[1] * row_open[None, :, None]
    mix_ext = coeff_ext[2]
    for step_index in range(NSUB):
        s = step_index
        e = east_ext.shape[1] - s
        w = east_ext.shape[2] - s
        tracer = advect_mix(
            tracer,
            east_ext[:, s:e, s:w],
            north_ext[:, s:e, s:w],
            mix_ext[:, s:e, s:w],
        )
    return tracer


def on_device(
    joint_tracer_field,
    courant_mixing_rates,
    oceanic_indicator,
    glacial_indicator,
    prior_oceanic_warmth,
    prior_glacial_cover,
    partner_devices,
    receiving_tile_index,
    bank_tile_entry,
    conservative_overlay_factors,
):
    owners = lax.axis_size("panel") * lax.axis_size("col")
    tile_count = partner_devices.shape[0]
    capacity = max(2, 4 * tile_count // owners)
    slots = owners * capacity
    nbank = conservative_overlay_factors.shape[0]
    on_atmos = lax.axis_index("comp") == 0
    device_tracer_share = joint_tracer_field[0]
    coeffs = courant_mixing_rates[0]
    grid_rows = coeffs.shape[2]
    grid_cols = coeffs.shape[3]
    sea_here = oceanic_indicator[0].astype(jnp.float32)
    wind_east = coeffs[0, 0]
    wind_north = coeffs[1, 0]
    airflow_speed = jnp.sqrt(wind_east * wind_east + wind_north * wind_north + 0.01)
    unfrozen_share = sea_here * (1.0 - prior_glacial_cover)
    thermal_exchange_rate = (
        2.0 * airflow_speed * (prior_oceanic_warmth - device_tracer_share[0, 0]) * unfrozen_share
    )
    evaporation_rate = (
        2.0
        * airflow_speed
        * (jnp.exp(0.1 * prior_oceanic_warmth) - device_tracer_share[1, 0])
        * unfrozen_share
    )
    heated = device_tracer_share.at[0, 0].add(thermal_exchange_rate).at[1, 0].add(evaporation_rate)
    start = jnp.where(on_atmos, heated, device_tracer_share)
    surface_flux = jnp.stack([thermal_exchange_rate, evaporation_rate])
    flux_rows = passed_along(to_tiles(surface_flux), "comp", 1).reshape(tile_count * 2, TILE)
    pairs = tile_count * 2

    bucket_place = bucket_places(partner_devices, owners, capacity)
    place_match = bucket_place[None, :] == jnp.arange(slots, dtype=jnp.int32)[:, None]
    slot_used = jnp.any(place_match, axis=1)
    slot_pair = jnp.sum(jnp.where(place_match, jnp.arange(pairs, dtype=jnp.int32)[None, :], 0), axis=1)
    slot_tile = slot_pair // 2
    slot_bank = jnp.sum(jnp.where(place_match, bank_tile_entry.reshape(-1)[None, :], 0), axis=1)

    by_bank = jnp.einsum(
        "bji,ri->brj", conservative_overlay_factors, flux_rows, precision=lax.Precision.HIGH
    ).reshape(nbank * pairs, TILE)
    f_ids = jnp.arange(2, dtype=jnp.int32)[None, :]
    slot_rows = (slot_bank * pairs + slot_tile * 2)[:, None] + f_ids
    picked = by_bank[slot_rows.reshape(-1)].reshape(slots, 2, TILE)
    buffer = jnp.where(slot_used[:, None, None], picked, 0.0).reshape(owners, capacity * 2, TILE)
    slot_label = jnp.sum(jnp.where(place_match, receiving_tile_index.reshape(-1)[None, :], 0), axis=1)
    label_row = jnp.pad(
        slot_label.reshape(owners, capacity).astype(jnp.float32), ((0, 0), (0, TILE - capacity))
    )
    bucket = jnp.concatenate([buffer, label_row[:, None, :]], axis=1)
    rows_out = capacity * 2 + 1
    arrived = lax.all_to_all(
        bucket.reshape(owners, rows_out * TILE), ("panel", "col"), 0, 0, tiled=True
    ).reshape(owners, rows_out, TILE)
    received = arrived[:, : capacity * 2].reshape(slots * 2, TILE)
    recv_slots = arrived[:, capacity * 2, :capacity].astype(jnp.int32).reshape(-1)

    row_ids = lax.broadcasted_iota(jnp.int32, (pairs, slots * 2), 0)
    col_ids = lax.broadcasted_iota(jnp.int32, (pairs, slots * 2), 1)
    recv_rep = jnp.broadcast_to(recv_slots[:, None], (slots, 2)).reshape(-1)
    slot_hit2 = (
        (recv_rep[None, :] == row_ids // 2) & (col_ids % 2 == row_ids % 2)
    ).astype(jnp.float32)
    summed = jnp.dot(slot_hit2, received, precision=HIGHEST)
    forcing = from_tiles(summed.reshape(tile_count, 2, TILE), grid_rows, grid_cols)

    tracer = advect(start, coeffs, grid_rows)
    forced = (
        tracer.at[0, 0]
        .add(-(0.5 * sea_here * forcing[0]))
        .at[1, 0]
        .add(0.5 * sea_here * forcing[1])
    )
    new_here = jnp.where(on_atmos, tracer, forced)
    sea_temp = new_here[0, 0]
    ice_cover = (
        glacial_indicator.astype(jnp.float32) * sea_here * jnp.clip(0.5 - sea_temp, 0.0, 1.0)
    )
    ocean_surface = jnp.stack([sea_temp, ice_cover])
    ocean_tiles = to_tiles(ocean_surface).reshape(pairs, TILE)
    reply = jnp.dot(slot_hit2.T, ocean_tiles, precision=HIGHEST).reshape(owners, capacity * 2, TILE)
    returned = lax.all_to_all(reply, ("panel", "col"), 0, 0, tiled=True).reshape(slots * 2, TILE)
    place_rep = jnp.broadcast_to(bucket_place[:, None], (pairs, 2)).reshape(-1)
    p_rows = lax.broadcasted_iota(jnp.int32, (pairs * 2, slots * 2), 0)
    p_cols = lax.broadcasted_iota(jnp.int32, (pairs * 2, slots * 2), 1)
    place_hit2 = ((place_rep[:, None] == p_cols // 2) & (p_cols % 2 == p_rows % 2)).astype(
        jnp.float32
    )
    values = jnp.dot(place_hit2, returned, precision=HIGHEST)

    by_bank_back = jnp.einsum(
        "rj,bji->bri", values, conservative_overlay_factors, precision=lax.Precision.HIGH
    ).reshape(nbank * pairs * 2, TILE)
    tile_ids = jnp.arange(tile_count, dtype=jnp.int32)[:, None]
    pair_rows = (bank_tile_entry * tile_count + tile_ids) * 4 + jnp.arange(2, dtype=jnp.int32)[None, :] * 2
    back_rows = pair_rows[:, :, None] + f_ids[:, None, :]
    numerator = jnp.sum(by_bank_back[back_rows.reshape(-1)].reshape(tile_count, 2, 2, TILE), axis=1)
    column_sums = jnp.sum(conservative_overlay_factors, axis=1)
    bank_ids = jnp.arange(nbank, dtype=jnp.int32)[None, :]
    bank_count = (bank_tile_entry[:, :1] == bank_ids).astype(jnp.float32) + (
        bank_tile_entry[:, 1:] == bank_ids
    ).astype(jnp.float32)
    denominator = jnp.dot(bank_count, column_sums, precision=HIGHEST)
    remap_back = numerator / denominator[:, None, :]
    remapped = passed_along(from_tiles(remap_back, grid_rows, grid_cols), "comp", -1)
    surface_here = jnp.where(on_atmos, remapped, ocean_surface)
    return (new_here[None], surface_here[None])


def solution(mesh):
    return jax.shard_map(
        on_device,
        mesh=mesh,
        in_specs=(
            P("comp", None, None, "col", "panel"),
            P("comp", None, None, "col", "panel"),
            P("comp", "col", "panel"),
            P("col", "panel"),
            P("col", "panel"),
            P("col", "panel"),
            P(("panel", "col"), None),
            P(("panel", "col"), None),
            P(("panel", "col"), None),
            P(),
        ),
        out_specs=(P("comp", None, None, "col", "panel"), P("comp", None, "col", "panel")),
        check_vma=False,
    )
```

```python
import jax
import jax.numpy as jnp
from jax import lax
from jax.sharding import PartitionSpec as P

TILE = 128
NSUB = 4
HIGHEST = lax.Precision.HIGHEST


def passed_along(value, axis, steps):
    count = lax.axis_size(axis)
    initial, last = (max(0, -steps), min(count, count - steps))
    return lax.ppermute(value, axis, [(source, source + steps) for source in range(initial, last)])


def from_behind(array, axis, by):
    count = lax.axis_size(axis)
    return lax.ppermute(array, axis, [(i, (i + by) % count) for i in range(count)])


def wide_halo(array, width):
    west = from_behind(array[..., -width:], "panel", 1)
    east = from_behind(array[..., :width], "panel", -1)
    array = jnp.concatenate([west, array, east], axis=-1)
    south = passed_along(array[..., -width:, :], "col", 1)
    north = passed_along(array[..., :width, :], "col", -1)
    return jnp.concatenate([south, array, north], axis=-2)


def vertical_mix(tracer, mixing):
    level_flux = mixing[:-1] * (tracer[:, 1:] - tracer[:, :-1])
    zero_level = jnp.zeros_like(tracer[:, :1])
    from_above = jnp.concatenate([level_flux, zero_level], axis=1)
    from_below = jnp.concatenate([zero_level, level_flux], axis=1)
    relaxation = jnp.concatenate(
        [jnp.zeros_like(tracer[:, :-1]), mixing[-1:] * tracer[:, -1:]], axis=1
    )
    return tracer + from_above - from_below - relaxation


def advect_mix(tracer, east_vel, north_vel, mixing):
    centre = tracer[..., 1:-1, 1:-1]
    vel_east = east_vel[:, 1:-1, 1:-1]
    vel_west = east_vel[:, 1:-1, :-2]
    vel_north = north_vel[:, 1:-1, 1:-1]
    vel_south = north_vel[:, :-2, 1:-1]
    flux_east = (
        jnp.maximum(vel_east, 0.0) * centre + jnp.minimum(vel_east, 0.0) * tracer[..., 1:-1, 2:]
    )
    flux_west = (
        jnp.maximum(vel_west, 0.0) * tracer[..., 1:-1, :-2] + jnp.minimum(vel_west, 0.0) * centre
    )
    flux_north = (
        jnp.maximum(vel_north, 0.0) * centre + jnp.minimum(vel_north, 0.0) * tracer[..., 2:, 1:-1]
    )
    flux_south = (
        jnp.maximum(vel_south, 0.0) * tracer[..., :-2, 1:-1] + jnp.minimum(vel_south, 0.0) * centre
    )
    advanced = centre - (flux_east - flux_west) - (flux_north - flux_south)
    return vertical_mix(advanced, mixing[:, 1:-1, 1:-1])


def to_tiles(field_grid):
    fcount, grid_rows, grid_cols = field_grid.shape
    blocks = field_grid.reshape(fcount, grid_rows, grid_cols // TILE, TILE)
    return blocks.transpose(1, 2, 0, 3).reshape(-1, fcount, TILE)


def from_tiles(tile_form, grid_rows, grid_cols):
    fcount = tile_form.shape[1]
    blocks = tile_form.reshape(grid_rows, grid_cols // TILE, fcount, TILE)
    return blocks.transpose(2, 0, 1, 3).reshape(fcount, grid_rows, grid_cols)


def bucket_places(partner_devices, owners, capacity):
    owner_list = partner_devices.reshape(-1)
    owner_hit = (owner_list[:, None] == jnp.arange(owners, dtype=jnp.int32)[None, :]).astype(
        jnp.int32
    )
    owner_rank = jnp.cumsum(owner_hit, axis=0) - owner_hit
    position = jnp.sum(owner_rank * owner_hit, axis=1)
    return owner_list * capacity + position


def advect(start, coeffs, grid_rows):
    fields = start.shape[0] * start.shape[1]
    both = jnp.concatenate([start.reshape((fields,) + start.shape[2:]), coeffs.reshape((-1,) + coeffs.shape[2:])])
    wide = wide_halo(both, NSUB)
    levels = coeffs.shape[1]
    tracer = wide[:fields].reshape(start.shape[:2] + wide.shape[1:])
    coeff_ext = wide[fields:].reshape((3, levels) + wide.shape[1:])
    rows_total = grid_rows * lax.axis_size("col")
    row_global = (
        lax.axis_index("col") * grid_rows
        + jnp.arange(grid_rows + 2 * NSUB, dtype=jnp.int32)
        - NSUB
    )
    row_open = ((row_global >= 0) & (row_global < rows_total - 1)).astype(jnp.float32)
    east_ext = coeff_ext[0]
    north_ext = coeff_ext[1] * row_open[None, :, None]
    mix_ext = coeff_ext[2]
    for step_index in range(NSUB):
        s = step_index
        e = east_ext.shape[1] - s
        w = east_ext.shape[2] - s
        tracer = advect_mix(
            tracer,
            east_ext[:, s:e, s:w],
            north_ext[:, s:e, s:w],
            mix_ext[:, s:e, s:w],
        )
    return tracer


def on_device(
    joint_tracer_field,
    courant_mixing_rates,
    oceanic_indicator,
    glacial_indicator,
    prior_oceanic_warmth,
    prior_glacial_cover,
    partner_devices,
    receiving_tile_index,
    bank_tile_entry,
    conservative_overlay_factors,
):
    owners = lax.axis_size("panel") * lax.axis_size("col")
    tile_count = partner_devices.shape[0]
    capacity = max(2, 4 * tile_count // owners)
    slots = owners * capacity
    nbank = conservative_overlay_factors.shape[0]
    on_atmos = lax.axis_index("comp") == 0
    device_tracer_share = joint_tracer_field[0]
    coeffs = courant_mixing_rates[0]
    grid_rows = coeffs.shape[2]
    grid_cols = coeffs.shape[3]
    sea_here = oceanic_indicator[0].astype(jnp.float32)
    wind_east = coeffs[0, 0]
    wind_north = coeffs[1, 0]
    airflow_speed = jnp.sqrt(wind_east * wind_east + wind_north * wind_north + 0.01)
    unfrozen_share = sea_here * (1.0 - prior_glacial_cover)
    thermal_exchange_rate = (
        2.0 * airflow_speed * (prior_oceanic_warmth - device_tracer_share[0, 0]) * unfrozen_share
    )
    evaporation_rate = (
        2.0
        * airflow_speed
        * (jnp.exp(0.1 * prior_oceanic_warmth) - device_tracer_share[1, 0])
        * unfrozen_share
    )
    heated = device_tracer_share.at[0, 0].add(thermal_exchange_rate).at[1, 0].add(evaporation_rate)
    start = jnp.where(on_atmos, heated, device_tracer_share)
    surface_flux = jnp.stack([thermal_exchange_rate, evaporation_rate])
    flux_rows = passed_along(to_tiles(surface_flux), "comp", 1).reshape(tile_count * 2, TILE)
    pairs = tile_count * 2

    bucket_place = bucket_places(partner_devices, owners, capacity)
    place_match = bucket_place[None, :] == jnp.arange(slots, dtype=jnp.int32)[:, None]
    slot_used = jnp.any(place_match, axis=1)
    slot_pair = jnp.sum(jnp.where(place_match, jnp.arange(pairs, dtype=jnp.int32)[None, :], 0), axis=1)
    slot_tile = slot_pair // 2
    slot_bank = jnp.sum(jnp.where(place_match, bank_tile_entry.reshape(-1)[None, :], 0), axis=1)

    by_bank = jnp.einsum(
        "bji,ri->brj", conservative_overlay_factors, flux_rows, precision=lax.Precision.HIGH
    ).reshape(nbank * pairs, TILE)
    f_ids = jnp.arange(2, dtype=jnp.int32)[None, :]
    slot_rows = (slot_bank * pairs + slot_tile * 2)[:, None] + f_ids
    picked = by_bank[slot_rows.reshape(-1)].reshape(slots, 2, TILE)
    buffer = jnp.where(slot_used[:, None, None], picked, 0.0).reshape(owners, capacity * 2, TILE)
    received = lax.all_to_all(buffer, ("panel", "col"), 0, 0, tiled=True).reshape(slots * 2, TILE)

    me = lax.axis_index("panel") * lax.axis_size("col") + lax.axis_index("col")
    own_routes = jnp.concatenate([partner_devices.T, receiving_tile_index.T], axis=0)
    owner_ids = jnp.arange(owners, dtype=jnp.int32)[:, None, None]
    routes = lax.psum(
        jnp.where(owner_ids == me, own_routes[None].astype(jnp.float32), 0.0), ("panel", "col")
    ).astype(jnp.int32)
    mine = [(routes[:, k] == me).astype(jnp.int32) for k in range(2)]
    per_tile = mine[0] + mine[1]
    before = jnp.cumsum(per_tile, axis=1) - per_tile
    rank = [before, before + mine[0]]
    recv_slots = jnp.stack(
        [
            sum(jnp.sum(mine[k] * (rank[k] == c) * routes[:, 2 + k], axis=1) for k in range(2))
            for c in range(capacity)
        ],
        axis=1,
    ).reshape(-1)
    row_ids = lax.broadcasted_iota(jnp.int32, (pairs, slots * 2), 0)
    col_ids = lax.broadcasted_iota(jnp.int32, (pairs, slots * 2), 1)
    recv_rep = jnp.broadcast_to(recv_slots[:, None], (slots, 2)).reshape(-1)
    slot_hit2 = (
        (recv_rep[None, :] == row_ids // 2) & (col_ids % 2 == row_ids % 2)
    ).astype(jnp.float32)
    summed = jnp.dot(slot_hit2, received, precision=HIGHEST)
    forcing = from_tiles(summed.reshape(tile_count, 2, TILE), grid_rows, grid_cols)

    tracer = advect(start, coeffs, grid_rows)
    forced = (
        tracer.at[0, 0]
        .add(-(0.5 * sea_here * forcing[0]))
        .at[1, 0]
        .add(0.5 * sea_here * forcing[1])
    )
    new_here = jnp.where(on_atmos, tracer, forced)
    sea_temp = new_here[0, 0]
    ice_cover = (
        glacial_indicator.astype(jnp.float32) * sea_here * jnp.clip(0.5 - sea_temp, 0.0, 1.0)
    )
    ocean_surface = jnp.stack([sea_temp, ice_cover])
    ocean_tiles = to_tiles(ocean_surface).reshape(pairs, TILE)
    reply = jnp.dot(slot_hit2.T, ocean_tiles, precision=HIGHEST).reshape(owners, capacity * 2, TILE)
    returned = lax.all_to_all(reply, ("panel", "col"), 0, 0, tiled=True).reshape(slots * 2, TILE)
    place_rep = jnp.broadcast_to(bucket_place[:, None], (pairs, 2)).reshape(-1)
    p_rows = lax.broadcasted_iota(jnp.int32, (pairs * 2, slots * 2), 0)
    p_cols = lax.broadcasted_iota(jnp.int32, (pairs * 2, slots * 2), 1)
    place_hit2 = ((place_rep[:, None] == p_cols // 2) & (p_cols % 2 == p_rows % 2)).astype(
        jnp.float32
    )
    values = jnp.dot(place_hit2, returned, precision=HIGHEST)

    by_bank_back = jnp.einsum(
        "rj,bji->bri", values, conservative_overlay_factors, precision=lax.Precision.HIGH
    ).reshape(nbank * pairs * 2, TILE)
    tile_ids = jnp.arange(tile_count, dtype=jnp.int32)[:, None]
    pair_rows = (bank_tile_entry * tile_count + tile_ids) * 4 + jnp.arange(2, dtype=jnp.int32)[None, :] * 2
    back_rows = pair_rows[:, :, None] + f_ids[:, None, :]
    numerator = jnp.sum(by_bank_back[back_rows.reshape(-1)].reshape(tile_count, 2, 2, TILE), axis=1)
    column_sums = jnp.sum(conservative_overlay_factors, axis=1)
    bank_ids = jnp.arange(nbank, dtype=jnp.int32)[None, :]
    bank_count = (bank_tile_entry[:, :1] == bank_ids).astype(jnp.float32) + (
        bank_tile_entry[:, 1:] == bank_ids
    ).astype(jnp.float32)
    denominator = jnp.dot(bank_count, column_sums, precision=HIGHEST)
    remap_back = numerator / denominator[:, None, :]
    remapped = passed_along(from_tiles(remap_back, grid_rows, grid_cols), "comp", -1)
    surface_here = jnp.where(on_atmos, remapped, ocean_surface)
    return (new_here[None], surface_here[None])


def solution(mesh):
    return jax.shard_map(
        on_device,
        mesh=mesh,
        in_specs=(
            P("comp", None, None, "col", "panel"),
            P("comp", None, None, "col", "panel"),
            P("comp", "col", "panel"),
            P("col", "panel"),
            P("col", "panel"),
            P("col", "panel"),
            P(("panel", "col"), None),
            P(("panel", "col"), None),
            P(("panel", "col"), None),
            P(),
        ),
        out_specs=(P("comp", None, None, "col", "panel"), P("comp", None, "col", "panel")),
        check_vma=False,
    )
```

```python
import jax
import jax.numpy as jnp
from jax import lax
from jax.sharding import PartitionSpec as P

TILE = 128
NSUB = 4
HIGHEST = lax.Precision.HIGHEST


def passed_along(value, axis, steps):
    count = lax.axis_size(axis)
    initial, last = (max(0, -steps), min(count, count - steps))
    return lax.ppermute(value, axis, [(source, source + steps) for source in range(initial, last)])


def from_behind(array, axis, by):
    count = lax.axis_size(axis)
    return lax.ppermute(array, axis, [(i, (i + by) % count) for i in range(count)])


def wide_halo(array, width):
    west = from_behind(array[..., -TILE:], "panel", 1)[..., -width:]
    east = from_behind(array[..., :TILE], "panel", -1)[..., :width]
    array = jnp.concatenate([west, array, east], axis=-1)
    south = passed_along(array[..., -width:, :], "col", 1)
    north = passed_along(array[..., :width, :], "col", -1)
    return jnp.concatenate([south, array, north], axis=-2)


def vertical_mix(tracer, mixing):
    level_flux = mixing[:-1] * (tracer[:, 1:] - tracer[:, :-1])
    zero_level = jnp.zeros_like(tracer[:, :1])
    from_above = jnp.concatenate([level_flux, zero_level], axis=1)
    from_below = jnp.concatenate([zero_level, level_flux], axis=1)
    relaxation = jnp.concatenate(
        [jnp.zeros_like(tracer[:, :-1]), mixing[-1:] * tracer[:, -1:]], axis=1
    )
    return tracer + from_above - from_below - relaxation


def advect_mix(tracer, east_vel, north_vel, mixing):
    centre = tracer[..., 1:-1, 1:-1]
    vel_east = east_vel[:, 1:-1, 1:-1]
    vel_west = east_vel[:, 1:-1, :-2]
    vel_north = north_vel[:, 1:-1, 1:-1]
    vel_south = north_vel[:, :-2, 1:-1]
    flux_east = (
        jnp.maximum(vel_east, 0.0) * centre + jnp.minimum(vel_east, 0.0) * tracer[..., 1:-1, 2:]
    )
    flux_west = (
        jnp.maximum(vel_west, 0.0) * tracer[..., 1:-1, :-2] + jnp.minimum(vel_west, 0.0) * centre
    )
    flux_north = (
        jnp.maximum(vel_north, 0.0) * centre + jnp.minimum(vel_north, 0.0) * tracer[..., 2:, 1:-1]
    )
    flux_south = (
        jnp.maximum(vel_south, 0.0) * tracer[..., :-2, 1:-1] + jnp.minimum(vel_south, 0.0) * centre
    )
    advanced = centre - (flux_east - flux_west) - (flux_north - flux_south)
    return vertical_mix(advanced, mixing[:, 1:-1, 1:-1])


def to_tiles(field_grid):
    fcount, grid_rows, grid_cols = field_grid.shape
    blocks = field_grid.reshape(fcount, grid_rows, grid_cols // TILE, TILE)
    return blocks.transpose(1, 2, 0, 3).reshape(-1, fcount, TILE)


def from_tiles(tile_form, grid_rows, grid_cols):
    fcount = tile_form.shape[1]
    blocks = tile_form.reshape(grid_rows, grid_cols // TILE, fcount, TILE)
    return blocks.transpose(2, 0, 1, 3).reshape(fcount, grid_rows, grid_cols)


def bucket_places(partner_devices, owners, capacity):
    owner_list = partner_devices.reshape(-1)
    owner_hit = (owner_list[:, None] == jnp.arange(owners, dtype=jnp.int32)[None, :]).astype(
        jnp.int32
    )
    owner_rank = jnp.cumsum(owner_hit, axis=0) - owner_hit
    position = jnp.sum(owner_rank * owner_hit, axis=1)
    return owner_list * capacity + position


def advect(start, coeffs, grid_rows):
    fields = start.shape[0] * start.shape[1]
    both = jnp.concatenate([start.reshape((fields,) + start.shape[2:]), coeffs.reshape((-1,) + coeffs.shape[2:])])
    wide = wide_halo(both, NSUB)
    levels = coeffs.shape[1]
    tracer = wide[:fields].reshape(start.shape[:2] + wide.shape[1:])
    coeff_ext = wide[fields:].reshape((3, levels) + wide.shape[1:])
    rows_total = grid_rows * lax.axis_size("col")
    row_global = (
        lax.axis_index("col") * grid_rows
        + jnp.arange(grid_rows + 2 * NSUB, dtype=jnp.int32)
        - NSUB
    )
    row_open = ((row_global >= 0) & (row_global < rows_total - 1)).astype(jnp.float32)
    east_ext = coeff_ext[0]
    north_ext = coeff_ext[1] * row_open[None, :, None]
    mix_ext = coeff_ext[2]
    for step_index in range(NSUB):
        s = step_index
        e = east_ext.shape[1] - s
        w = east_ext.shape[2] - s
        tracer = advect_mix(
            tracer,
            east_ext[:, s:e, s:w],
            north_ext[:, s:e, s:w],
            mix_ext[:, s:e, s:w],
        )
    return tracer


def on_device(
    joint_tracer_field,
    courant_mixing_rates,
    oceanic_indicator,
    glacial_indicator,
    prior_oceanic_warmth,
    prior_glacial_cover,
    partner_devices,
    receiving_tile_index,
    bank_tile_entry,
    conservative_overlay_factors,
):
    owners = lax.axis_size("panel") * lax.axis_size("col")
    tile_count = partner_devices.shape[0]
    capacity = max(2, 4 * tile_count // owners)
    slots = owners * capacity
    nbank = conservative_overlay_factors.shape[0]
    on_atmos = lax.axis_index("comp") == 0
    device_tracer_share = joint_tracer_field[0]
    coeffs = courant_mixing_rates[0]
    grid_rows = coeffs.shape[2]
    grid_cols = coeffs.shape[3]
    sea_here = oceanic_indicator[0].astype(jnp.float32)
    wind_east = coeffs[0, 0]
    wind_north = coeffs[1, 0]
    airflow_speed = jnp.sqrt(wind_east * wind_east + wind_north * wind_north + 0.01)
    unfrozen_share = sea_here * (1.0 - prior_glacial_cover)
    thermal_exchange_rate = (
        2.0 * airflow_speed * (prior_oceanic_warmth - device_tracer_share[0, 0]) * unfrozen_share
    )
    evaporation_rate = (
        2.0
        * airflow_speed
        * (jnp.exp(0.1 * prior_oceanic_warmth) - device_tracer_share[1, 0])
        * unfrozen_share
    )
    heated = device_tracer_share.at[0, 0].add(thermal_exchange_rate).at[1, 0].add(evaporation_rate)
    start = jnp.where(on_atmos, heated, device_tracer_share)
    surface_flux = jnp.stack([thermal_exchange_rate, evaporation_rate])
    flux_rows = passed_along(to_tiles(surface_flux), "comp", 1).reshape(tile_count * 2, TILE)
    pairs = tile_count * 2

    bucket_place = bucket_places(partner_devices, owners, capacity)
    place_match = bucket_place[None, :] == jnp.arange(slots, dtype=jnp.int32)[:, None]
    slot_used = jnp.any(place_match, axis=1)
    slot_pair = jnp.sum(jnp.where(place_match, jnp.arange(pairs, dtype=jnp.int32)[None, :], 0), axis=1)
    slot_tile = slot_pair // 2
    slot_bank = jnp.sum(jnp.where(place_match, bank_tile_entry.reshape(-1)[None, :], 0), axis=1)

    by_bank = jnp.einsum(
        "bji,ri->brj", conservative_overlay_factors, flux_rows, precision=lax.Precision.HIGH
    ).reshape(nbank * pairs, TILE)
    f_ids = jnp.arange(2, dtype=jnp.int32)[None, :]
    slot_rows = (slot_bank * pairs + slot_tile * 2)[:, None] + f_ids
    picked = by_bank[slot_rows.reshape(-1)].reshape(slots, 2, TILE)
    buffer = jnp.where(slot_used[:, None, None], picked, 0.0).reshape(owners, capacity * 2, TILE)
    slot_label = jnp.sum(jnp.where(place_match, receiving_tile_index.reshape(-1)[None, :], 0), axis=1)
    label_row = jnp.pad(
        slot_label.reshape(owners, capacity).astype(jnp.float32), ((0, 0), (0, TILE - capacity))
    )
    bucket = jnp.concatenate([buffer, label_row[:, None, :]], axis=1)
    rows_out = capacity * 2 + 1
    arrived = lax.all_to_all(
        bucket.reshape(owners, rows_out * TILE), ("panel", "col"), 0, 0, tiled=True
    ).reshape(owners, rows_out, TILE)
    received = arrived[:, : capacity * 2].reshape(slots * 2, TILE)
    recv_slots = arrived[:, capacity * 2, :capacity].astype(jnp.int32).reshape(-1)

    row_ids = lax.broadcasted_iota(jnp.int32, (pairs, slots * 2), 0)
    col_ids = lax.broadcasted_iota(jnp.int32, (pairs, slots * 2), 1)
    recv_rep = jnp.broadcast_to(recv_slots[:, None], (slots, 2)).reshape(-1)
    slot_hit2 = (
        (recv_rep[None, :] == row_ids // 2) & (col_ids % 2 == row_ids % 2)
    ).astype(jnp.float32)
    summed = jnp.dot(slot_hit2, received, precision=HIGHEST)
    forcing = from_tiles(summed.reshape(tile_count, 2, TILE), grid_rows, grid_cols)

    tracer = advect(start, coeffs, grid_rows)
    forced = (
        tracer.at[0, 0]
        .add(-(0.5 * sea_here * forcing[0]))
        .at[1, 0]
        .add(0.5 * sea_here * forcing[1])
    )
    new_here = jnp.where(on_atmos, tracer, forced)
    sea_temp = new_here[0, 0]
    ice_cover = (
        glacial_indicator.astype(jnp.float32) * sea_here * jnp.clip(0.5 - sea_temp, 0.0, 1.0)
    )
    ocean_surface = jnp.stack([sea_temp, ice_cover])
    ocean_tiles = to_tiles(ocean_surface).reshape(pairs, TILE)
    reply = jnp.dot(slot_hit2.T, ocean_tiles, precision=HIGHEST).reshape(owners, capacity * 2, TILE)
    returned = lax.all_to_all(reply, ("panel", "col"), 0, 0, tiled=True).reshape(slots * 2, TILE)
    place_rep = jnp.broadcast_to(bucket_place[:, None], (pairs, 2)).reshape(-1)
    p_rows = lax.broadcasted_iota(jnp.int32, (pairs * 2, slots * 2), 0)
    p_cols = lax.broadcasted_iota(jnp.int32, (pairs * 2, slots * 2), 1)
    place_hit2 = ((place_rep[:, None] == p_cols // 2) & (p_cols % 2 == p_rows % 2)).astype(
        jnp.float32
    )
    values = jnp.dot(place_hit2, returned, precision=HIGHEST)

    by_bank_back = jnp.einsum(
        "rj,bji->bri", values, conservative_overlay_factors, precision=lax.Precision.HIGH
    ).reshape(nbank * pairs * 2, TILE)
    tile_ids = jnp.arange(tile_count, dtype=jnp.int32)[:, None]
    pair_rows = (bank_tile_entry * tile_count + tile_ids) * 4 + jnp.arange(2, dtype=jnp.int32)[None, :] * 2
    back_rows = pair_rows[:, :, None] + f_ids[:, None, :]
    numerator = jnp.sum(by_bank_back[back_rows.reshape(-1)].reshape(tile_count, 2, 2, TILE), axis=1)
    column_sums = jnp.sum(conservative_overlay_factors, axis=1)
    bank_ids = jnp.arange(nbank, dtype=jnp.int32)[None, :]
    bank_count = (bank_tile_entry[:, :1] == bank_ids).astype(jnp.float32) + (
        bank_tile_entry[:, 1:] == bank_ids
    ).astype(jnp.float32)
    denominator = jnp.dot(bank_count, column_sums, precision=HIGHEST)
    remap_back = numerator / denominator[:, None, :]
    remapped = passed_along(from_tiles(remap_back, grid_rows, grid_cols), "comp", -1)
    surface_here = jnp.where(on_atmos, remapped, ocean_surface)
    return (new_here[None], surface_here[None])


def solution(mesh):
    return jax.shard_map(
        on_device,
        mesh=mesh,
        in_specs=(
            P("comp", None, None, "col", "panel"),
            P("comp", None, None, "col", "panel"),
            P("comp", "col", "panel"),
            P("col", "panel"),
            P("col", "panel"),
            P("col", "panel"),
            P(("panel", "col"), None),
            P(("panel", "col"), None),
            P(("panel", "col"), None),
            P(),
        ),
        out_specs=(P("comp", None, None, "col", "panel"), P("comp", None, "col", "panel")),
        check_vma=False,
    )
```

```python
import jax
import jax.numpy as jnp
from jax import lax
from jax.sharding import PartitionSpec as P

TILE = 128
NSUB = 4
HIGHEST = lax.Precision.HIGHEST


def passed_along(value, axis, steps):
    count = lax.axis_size(axis)
    initial, last = (max(0, -steps), min(count, count - steps))
    return lax.ppermute(value, axis, [(source, source + steps) for source in range(initial, last)])


def from_behind(array, axis, by):
    count = lax.axis_size(axis)
    return lax.ppermute(array, axis, [(i, (i + by) % count) for i in range(count)])


def wide_halo(array, width):
    west = from_behind(array[..., -TILE:], "panel", 1)[..., -width:]
    east = from_behind(array[..., :TILE], "panel", -1)[..., :width]
    array = jnp.concatenate([west, array, east], axis=-1)
    south = passed_along(array[..., -width:, :], "col", 1)
    north = passed_along(array[..., :width, :], "col", -1)
    return jnp.concatenate([south, array, north], axis=-2)


def vertical_mix(tracer, mixing):
    level_flux = mixing[:-1] * (tracer[:, 1:] - tracer[:, :-1])
    zero_level = jnp.zeros_like(tracer[:, :1])
    from_above = jnp.concatenate([level_flux, zero_level], axis=1)
    from_below = jnp.concatenate([zero_level, level_flux], axis=1)
    relaxation = jnp.concatenate(
        [jnp.zeros_like(tracer[:, :-1]), mixing[-1:] * tracer[:, -1:]], axis=1
    )
    return tracer + from_above - from_below - relaxation


def advect_mix(tracer, east_vel, north_vel, mixing):
    centre = tracer[..., 1:-1, 1:-1]
    vel_east = east_vel[:, 1:-1, 1:-1]
    vel_west = east_vel[:, 1:-1, :-2]
    vel_north = north_vel[:, 1:-1, 1:-1]
    vel_south = north_vel[:, :-2, 1:-1]
    flux_east = (
        jnp.maximum(vel_east, 0.0) * centre + jnp.minimum(vel_east, 0.0) * tracer[..., 1:-1, 2:]
    )
    flux_west = (
        jnp.maximum(vel_west, 0.0) * tracer[..., 1:-1, :-2] + jnp.minimum(vel_west, 0.0) * centre
    )
    flux_north = (
        jnp.maximum(vel_north, 0.0) * centre + jnp.minimum(vel_north, 0.0) * tracer[..., 2:, 1:-1]
    )
    flux_south = (
        jnp.maximum(vel_south, 0.0) * tracer[..., :-2, 1:-1] + jnp.minimum(vel_south, 0.0) * centre
    )
    advanced = centre - (flux_east - flux_west) - (flux_north - flux_south)
    return vertical_mix(advanced, mixing[:, 1:-1, 1:-1])


def to_tiles(field_grid):
    fcount, grid_rows, grid_cols = field_grid.shape
    blocks = field_grid.reshape(fcount, grid_rows, grid_cols // TILE, TILE)
    return blocks.transpose(1, 2, 0, 3).reshape(-1, fcount, TILE)


def from_tiles(tile_form, grid_rows, grid_cols):
    fcount = tile_form.shape[1]
    blocks = tile_form.reshape(grid_rows, grid_cols // TILE, fcount, TILE)
    return blocks.transpose(2, 0, 1, 3).reshape(fcount, grid_rows, grid_cols)


def bucket_places(partner_devices, owners, capacity):
    owner_list = partner_devices.reshape(-1)
    owner_hit = (owner_list[:, None] == jnp.arange(owners, dtype=jnp.int32)[None, :]).astype(
        jnp.int32
    )
    owner_rank = jnp.cumsum(owner_hit, axis=0) - owner_hit
    position = jnp.sum(owner_rank * owner_hit, axis=1)
    return owner_list * capacity + position


def advect(start, coeffs, grid_rows):
    fields = start.shape[0] * start.shape[1]
    both = jnp.concatenate([start.reshape((fields,) + start.shape[2:]), coeffs.reshape((-1,) + coeffs.shape[2:])])
    wide = wide_halo(both, NSUB)
    levels = coeffs.shape[1]
    tracer = wide[:fields].reshape(start.shape[:2] + wide.shape[1:])
    coeff_ext = wide[fields:].reshape((3, levels) + wide.shape[1:])
    rows_total = grid_rows * lax.axis_size("col")
    row_global = (
        lax.axis_index("col") * grid_rows
        + jnp.arange(grid_rows + 2 * NSUB, dtype=jnp.int32)
        - NSUB
    )
    row_open = ((row_global >= 0) & (row_global < rows_total - 1)).astype(jnp.float32)
    east_ext = coeff_ext[0]
    north_ext = coeff_ext[1] * row_open[None, :, None]
    mix_ext = coeff_ext[2]
    for step_index in range(NSUB):
        s = step_index
        e = east_ext.shape[1] - s
        w = east_ext.shape[2] - s
        tracer = advect_mix(
            tracer,
            east_ext[:, s:e, s:w],
            north_ext[:, s:e, s:w],
            mix_ext[:, s:e, s:w],
        )
    return tracer


def on_device(
    joint_tracer_field,
    courant_mixing_rates,
    oceanic_indicator,
    glacial_indicator,
    prior_oceanic_warmth,
    prior_glacial_cover,
    partner_devices,
    receiving_tile_index,
    bank_tile_entry,
    conservative_overlay_factors,
):
    owners = lax.axis_size("panel") * lax.axis_size("col")
    tile_count = partner_devices.shape[0]
    capacity = max(2, 4 * tile_count // owners)
    slots = owners * capacity
    nbank = conservative_overlay_factors.shape[0]
    on_atmos = lax.axis_index("comp") == 0
    device_tracer_share = joint_tracer_field[0]
    coeffs = courant_mixing_rates[0]
    grid_rows = coeffs.shape[2]
    grid_cols = coeffs.shape[3]
    sea_here = oceanic_indicator[0].astype(jnp.float32)
    wind_east = coeffs[0, 0]
    wind_north = coeffs[1, 0]
    airflow_speed = jnp.sqrt(wind_east * wind_east + wind_north * wind_north + 0.01)
    unfrozen_share = sea_here * (1.0 - prior_glacial_cover)
    thermal_exchange_rate = (
        2.0 * airflow_speed * (prior_oceanic_warmth - device_tracer_share[0, 0]) * unfrozen_share
    )
    evaporation_rate = (
        2.0
        * airflow_speed
        * (jnp.exp(0.1 * prior_oceanic_warmth) - device_tracer_share[1, 0])
        * unfrozen_share
    )
    heated = device_tracer_share.at[0, 0].add(thermal_exchange_rate).at[1, 0].add(evaporation_rate)
    start = jnp.where(on_atmos, heated, device_tracer_share)
    surface_flux = jnp.stack([thermal_exchange_rate, evaporation_rate])
    flux_rows = passed_along(to_tiles(surface_flux), "comp", 1).reshape(tile_count * 2, TILE)
    pairs = tile_count * 2

    bucket_place = bucket_places(partner_devices, owners, capacity)
    place_match = bucket_place[None, :] == jnp.arange(slots, dtype=jnp.int32)[:, None]
    place_rep = jnp.broadcast_to(bucket_place[:, None], (pairs, 2)).reshape(-1)
    p_rows = lax.broadcasted_iota(jnp.int32, (pairs * 2, slots * 2), 0)
    p_cols = lax.broadcasted_iota(jnp.int32, (pairs * 2, slots * 2), 1)
    place_hit2 = ((place_rep[:, None] == p_cols // 2) & (p_cols % 2 == p_rows % 2)).astype(
        jnp.float32
    )

    by_bank = jnp.einsum(
        "bji,ri->brj", conservative_overlay_factors, flux_rows, precision=lax.Precision.HIGH
    ).reshape(nbank * pairs, TILE)
    f_ids = jnp.arange(2, dtype=jnp.int32)[None, :]
    tile_ids = jnp.arange(tile_count, dtype=jnp.int32)[:, None]
    spread_rows = (bank_tile_entry * pairs + tile_ids * 2)[:, :, None] + f_ids[:, None, :]
    contrib = by_bank[spread_rows.reshape(-1)]
    buffer = jnp.dot(place_hit2.T, contrib, precision=HIGHEST).reshape(owners, capacity * 2, TILE)
    slot_label = jnp.sum(jnp.where(place_match, receiving_tile_index.reshape(-1)[None, :], 0), axis=1)
    label_row = jnp.pad(
        slot_label.reshape(owners, capacity).astype(jnp.float32), ((0, 0), (0, TILE - capacity))
    )
    bucket = jnp.concatenate([buffer, label_row[:, None, :]], axis=1)
    rows_out = capacity * 2 + 1
    arrived = lax.all_to_all(
        bucket.reshape(owners, rows_out * TILE), ("panel", "col"), 0, 0, tiled=True
    ).reshape(owners, rows_out, TILE)
    received = arrived[:, : capacity * 2].reshape(slots * 2, TILE)
    recv_slots = arrived[:, capacity * 2, :capacity].astype(jnp.int32).reshape(-1)

    row_ids = lax.broadcasted_iota(jnp.int32, (pairs, slots * 2), 0)
    col_ids = lax.broadcasted_iota(jnp.int32, (pairs, slots * 2), 1)
    recv_rep = jnp.broadcast_to(recv_slots[:, None], (slots, 2)).reshape(-1)
    slot_hit2 = (
        (recv_rep[None, :] == row_ids // 2) & (col_ids % 2 == row_ids % 2)
    ).astype(jnp.float32)
    summed = jnp.dot(slot_hit2, received, precision=HIGHEST)
    forcing = from_tiles(summed.reshape(tile_count, 2, TILE), grid_rows, grid_cols)

    tracer = advect(start, coeffs, grid_rows)
    forced = (
        tracer.at[0, 0]
        .add(-(0.5 * sea_here * forcing[0]))
        .at[1, 0]
        .add(0.5 * sea_here * forcing[1])
    )
    new_here = jnp.where(on_atmos, tracer, forced)
    sea_temp = new_here[0, 0]
    ice_cover = (
        glacial_indicator.astype(jnp.float32) * sea_here * jnp.clip(0.5 - sea_temp, 0.0, 1.0)
    )
    ocean_surface = jnp.stack([sea_temp, ice_cover])
    ocean_tiles = to_tiles(ocean_surface).reshape(pairs, TILE)
    reply = jnp.dot(slot_hit2.T, ocean_tiles, precision=HIGHEST).reshape(owners, capacity * 2, TILE)
    returned = lax.all_to_all(reply, ("panel", "col"), 0, 0, tiled=True).reshape(slots * 2, TILE)
    values = jnp.dot(place_hit2, returned, precision=HIGHEST)

    by_bank_back = jnp.einsum(
        "rj,bji->bri", values, conservative_overlay_factors, precision=lax.Precision.HIGH
    ).reshape(nbank * pairs * 2, TILE)
    pair_rows = (bank_tile_entry * tile_count + tile_ids) * 4 + jnp.arange(2, dtype=jnp.int32)[None, :] * 2
    back_rows = pair_rows[:, :, None] + f_ids[:, None, :]
    numerator = jnp.sum(by_bank_back[back_rows.reshape(-1)].reshape(tile_count, 2, 2, TILE), axis=1)
    column_sums = jnp.sum(conservative_overlay_factors, axis=1)
    bank_ids = jnp.arange(nbank, dtype=jnp.int32)[None, :]
    bank_count = (bank_tile_entry[:, :1] == bank_ids).astype(jnp.float32) + (
        bank_tile_entry[:, 1:] == bank_ids
    ).astype(jnp.float32)
    denominator = jnp.dot(bank_count, column_sums, precision=HIGHEST)
    remap_back = numerator / denominator[:, None, :]
    remapped = passed_along(from_tiles(remap_back, grid_rows, grid_cols), "comp", -1)
    surface_here = jnp.where(on_atmos, remapped, ocean_surface)
    return (new_here[None], surface_here[None])


def solution(mesh):
    return jax.shard_map(
        on_device,
        mesh=mesh,
        in_specs=(
            P("comp", None, None, "col", "panel"),
            P("comp", None, None, "col", "panel"),
            P("comp", "col", "panel"),
            P("col", "panel"),
            P("col", "panel"),
            P("col", "panel"),
            P(("panel", "col"), None),
            P(("panel", "col"), None),
            P(("panel", "col"), None),
            P(),
        ),
        out_specs=(P("comp", None, None, "col", "panel"), P("comp", None, "col", "panel")),
        check_vma=False,
    )
```

```python
import jax
import jax.numpy as jnp
from jax import lax
from jax.sharding import PartitionSpec as P

TILE = 128
NSUB = 4
HIGHEST = lax.Precision.HIGHEST


def passed_along(value, axis, steps):
    count = lax.axis_size(axis)
    initial, last = (max(0, -steps), min(count, count - steps))
    return lax.ppermute(value, axis, [(source, source + steps) for source in range(initial, last)])


def from_behind(array, axis, by):
    count = lax.axis_size(axis)
    return lax.ppermute(array, axis, [(i, (i + by) % count) for i in range(count)])


def wide_halo(array, width):
    south = passed_along(array[..., -8:, :], "col", 1)[..., -width:, :]
    north = passed_along(array[..., :8, :], "col", -1)[..., :width, :]
    array = jnp.concatenate([south, array, north], axis=-2)
    west = from_behind(array[..., -TILE:], "panel", 1)[..., -width:]
    east = from_behind(array[..., :TILE], "panel", -1)[..., :width]
    return jnp.concatenate([west, array, east], axis=-1)


def vertical_mix(tracer, mixing):
    level_flux = mixing[:-1] * (tracer[:, 1:] - tracer[:, :-1])
    zero_level = jnp.zeros_like(tracer[:, :1])
    from_above = jnp.concatenate([level_flux, zero_level], axis=1)
    from_below = jnp.concatenate([zero_level, level_flux], axis=1)
    relaxation = jnp.concatenate(
        [jnp.zeros_like(tracer[:, :-1]), mixing[-1:] * tracer[:, -1:]], axis=1
    )
    return tracer + from_above - from_below - relaxation


def advect_mix(tracer, east_vel, north_vel, mixing):
    centre = tracer[..., 1:-1, 1:-1]
    vel_east = east_vel[:, 1:-1, 1:-1]
    vel_west = east_vel[:, 1:-1, :-2]
    vel_north = north_vel[:, 1:-1, 1:-1]
    vel_south = north_vel[:, :-2, 1:-1]
    flux_east = (
        jnp.maximum(vel_east, 0.0) * centre + jnp.minimum(vel_east, 0.0) * tracer[..., 1:-1, 2:]
    )
    flux_west = (
        jnp.maximum(vel_west, 0.0) * tracer[..., 1:-1, :-2] + jnp.minimum(vel_west, 0.0) * centre
    )
    flux_north = (
        jnp.maximum(vel_north, 0.0) * centre + jnp.minimum(vel_north, 0.0) * tracer[..., 2:, 1:-1]
    )
    flux_south = (
        jnp.maximum(vel_south, 0.0) * tracer[..., :-2, 1:-1] + jnp.minimum(vel_south, 0.0) * centre
    )
    advanced = centre - (flux_east - flux_west) - (flux_north - flux_south)
    return vertical_mix(advanced, mixing[:, 1:-1, 1:-1])


def to_tiles(field_grid):
    fcount, grid_rows, grid_cols = field_grid.shape
    blocks = field_grid.reshape(fcount, grid_rows, grid_cols // TILE, TILE)
    return blocks.transpose(1, 2, 0, 3).reshape(-1, fcount, TILE)


def from_tiles(tile_form, grid_rows, grid_cols):
    fcount = tile_form.shape[1]
    blocks = tile_form.reshape(grid_rows, grid_cols // TILE, fcount, TILE)
    return blocks.transpose(2, 0, 1, 3).reshape(fcount, grid_rows, grid_cols)


def bucket_places(partner_devices, owners, capacity):
    owner_list = partner_devices.reshape(-1)
    owner_hit = (owner_list[:, None] == jnp.arange(owners, dtype=jnp.int32)[None, :]).astype(
        jnp.int32
    )
    owner_rank = jnp.cumsum(owner_hit, axis=0) - owner_hit
    position = jnp.sum(owner_rank * owner_hit, axis=1)
    return owner_list * capacity + position


def advect(start, coeffs, grid_rows):
    fields = start.shape[0] * start.shape[1]
    both = jnp.concatenate([start.reshape((fields,) + start.shape[2:]), coeffs.reshape((-1,) + coeffs.shape[2:])])
    wide = wide_halo(both, NSUB)
    levels = coeffs.shape[1]
    tracer = wide[:fields].reshape(start.shape[:2] + wide.shape[1:])
    coeff_ext = wide[fields:].reshape((3, levels) + wide.shape[1:])
    rows_total = grid_rows * lax.axis_size("col")
    row_global = (
        lax.axis_index("col") * grid_rows
        + jnp.arange(grid_rows + 2 * NSUB, dtype=jnp.int32)
        - NSUB
    )
    row_open = ((row_global >= 0) & (row_global < rows_total - 1)).astype(jnp.float32)
    east_ext = coeff_ext[0]
    north_ext = coeff_ext[1] * row_open[None, :, None]
    mix_ext = coeff_ext[2]
    for step_index in range(NSUB):
        s = step_index
        e = east_ext.shape[1] - s
        w = east_ext.shape[2] - s
        tracer = advect_mix(
            tracer,
            east_ext[:, s:e, s:w],
            north_ext[:, s:e, s:w],
            mix_ext[:, s:e, s:w],
        )
    return tracer


def on_device(
    joint_tracer_field,
    courant_mixing_rates,
    oceanic_indicator,
    glacial_indicator,
    prior_oceanic_warmth,
    prior_glacial_cover,
    partner_devices,
    receiving_tile_index,
    bank_tile_entry,
    conservative_overlay_factors,
):
    owners = lax.axis_size("panel") * lax.axis_size("col")
    tile_count = partner_devices.shape[0]
    capacity = max(2, 4 * tile_count // owners)
    slots = owners * capacity
    nbank = conservative_overlay_factors.shape[0]
    on_atmos = lax.axis_index("comp") == 0
    device_tracer_share = joint_tracer_field[0]
    coeffs = courant_mixing_rates[0]
    grid_rows = coeffs.shape[2]
    grid_cols = coeffs.shape[3]
    sea_here = oceanic_indicator[0].astype(jnp.float32)
    wind_east = coeffs[0, 0]
    wind_north = coeffs[1, 0]
    airflow_speed = jnp.sqrt(wind_east * wind_east + wind_north * wind_north + 0.01)
    unfrozen_share = sea_here * (1.0 - prior_glacial_cover)
    thermal_exchange_rate = (
        2.0 * airflow_speed * (prior_oceanic_warmth - device_tracer_share[0, 0]) * unfrozen_share
    )
    evaporation_rate = (
        2.0
        * airflow_speed
        * (jnp.exp(0.1 * prior_oceanic_warmth) - device_tracer_share[1, 0])
        * unfrozen_share
    )
    heated = device_tracer_share.at[0, 0].add(thermal_exchange_rate).at[1, 0].add(evaporation_rate)
    start = jnp.where(on_atmos, heated, device_tracer_share)
    surface_flux = jnp.stack([thermal_exchange_rate, evaporation_rate])
    flux_rows = passed_along(to_tiles(surface_flux), "comp", 1).reshape(tile_count * 2, TILE)
    pairs = tile_count * 2

    bucket_place = bucket_places(partner_devices, owners, capacity)
    place_match = bucket_place[None, :] == jnp.arange(slots, dtype=jnp.int32)[:, None]
    slot_used = jnp.any(place_match, axis=1)
    slot_pair = jnp.sum(jnp.where(place_match, jnp.arange(pairs, dtype=jnp.int32)[None, :], 0), axis=1)
    slot_tile = slot_pair // 2
    slot_bank = jnp.sum(jnp.where(place_match, bank_tile_entry.reshape(-1)[None, :], 0), axis=1)

    by_bank = jnp.einsum(
        "bji,ri->brj", conservative_overlay_factors, flux_rows, precision=lax.Precision.HIGH
    ).reshape(nbank * pairs, TILE)
    f_ids = jnp.arange(2, dtype=jnp.int32)[None, :]
    slot_rows = (slot_bank * pairs + slot_tile * 2)[:, None] + f_ids
    picked = by_bank[slot_rows.reshape(-1)].reshape(slots, 2, TILE)
    buffer = jnp.where(slot_used[:, None, None], picked, 0.0).reshape(owners, capacity * 2, TILE)
    slot_label = jnp.sum(jnp.where(place_match, receiving_tile_index.reshape(-1)[None, :], 0), axis=1)
    label_row = jnp.pad(
        slot_label.reshape(owners, capacity).astype(jnp.float32), ((0, 0), (0, TILE - capacity))
    )
    bucket = jnp.concatenate([buffer, label_row[:, None, :]], axis=1)
    rows_out = capacity * 2 + 1
    arrived = lax.all_to_all(
        bucket.reshape(owners, rows_out * TILE), ("panel", "col"), 0, 0, tiled=True
    ).reshape(owners, rows_out, TILE)
    received = arrived[:, : capacity * 2].reshape(slots * 2, TILE)
    recv_slots = arrived[:, capacity * 2, :capacity].astype(jnp.int32).reshape(-1)

    row_ids = lax.broadcasted_iota(jnp.int32, (pairs, slots * 2), 0)
    col_ids = lax.broadcasted_iota(jnp.int32, (pairs, slots * 2), 1)
    recv_rep = jnp.broadcast_to(recv_slots[:, None], (slots, 2)).reshape(-1)
    slot_hit2 = (
        (recv_rep[None, :] == row_ids // 2) & (col_ids % 2 == row_ids % 2)
    ).astype(jnp.float32)
    summed = jnp.dot(slot_hit2, received, precision=HIGHEST)
    forcing = from_tiles(summed.reshape(tile_count, 2, TILE), grid_rows, grid_cols)

    tracer = advect(start, coeffs, grid_rows)
    forced = (
        tracer.at[0, 0]
        .add(-(0.5 * sea_here * forcing[0]))
        .at[1, 0]
        .add(0.5 * sea_here * forcing[1])
    )
    new_here = jnp.where(on_atmos, tracer, forced)
    sea_temp = new_here[0, 0]
    ice_cover = (
        glacial_indicator.astype(jnp.float32) * sea_here * jnp.clip(0.5 - sea_temp, 0.0, 1.0)
    )
    ocean_surface = jnp.stack([sea_temp, ice_cover])
    ocean_tiles = to_tiles(ocean_surface).reshape(pairs, TILE)
    reply = jnp.dot(slot_hit2.T, ocean_tiles, precision=HIGHEST).reshape(owners, capacity * 2, TILE)
    returned = lax.all_to_all(reply, ("panel", "col"), 0, 0, tiled=True).reshape(slots * 2, TILE)
    place_rep = jnp.broadcast_to(bucket_place[:, None], (pairs, 2)).reshape(-1)
    p_rows = lax.broadcasted_iota(jnp.int32, (pairs * 2, slots * 2), 0)
    p_cols = lax.broadcasted_iota(jnp.int32, (pairs * 2, slots * 2), 1)
    place_hit2 = ((place_rep[:, None] == p_cols // 2) & (p_cols % 2 == p_rows % 2)).astype(
        jnp.float32
    )
    values = jnp.dot(place_hit2, returned, precision=HIGHEST)

    by_bank_back = jnp.einsum(
        "rj,bji->bri", values, conservative_overlay_factors, precision=lax.Precision.HIGH
    ).reshape(nbank * pairs * 2, TILE)
    tile_ids = jnp.arange(tile_count, dtype=jnp.int32)[:, None]
    pair_rows = (bank_tile_entry * tile_count + tile_ids) * 4 + jnp.arange(2, dtype=jnp.int32)[None, :] * 2
    back_rows = pair_rows[:, :, None] + f_ids[:, None, :]
    numerator = jnp.sum(by_bank_back[back_rows.reshape(-1)].reshape(tile_count, 2, 2, TILE), axis=1)
    column_sums = jnp.sum(conservative_overlay_factors, axis=1)
    bank_ids = jnp.arange(nbank, dtype=jnp.int32)[None, :]
    bank_count = (bank_tile_entry[:, :1] == bank_ids).astype(jnp.float32) + (
        bank_tile_entry[:, 1:] == bank_ids
    ).astype(jnp.float32)
    denominator = jnp.dot(bank_count, column_sums, precision=HIGHEST)
    remap_back = numerator / denominator[:, None, :]
    remapped = passed_along(from_tiles(remap_back, grid_rows, grid_cols), "comp", -1)
    surface_here = jnp.where(on_atmos, remapped, ocean_surface)
    return (new_here[None], surface_here[None])


def solution(mesh):
    return jax.shard_map(
        on_device,
        mesh=mesh,
        in_specs=(
            P("comp", None, None, "col", "panel"),
            P("comp", None, None, "col", "panel"),
            P("comp", "col", "panel"),
            P("col", "panel"),
            P("col", "panel"),
            P("col", "panel"),
            P(("panel", "col"), None),
            P(("panel", "col"), None),
            P(("panel", "col"), None),
            P(),
        ),
        out_specs=(P("comp", None, None, "col", "panel"), P("comp", None, "col", "panel")),
        check_vma=False,
    )
```

```python
import jax
import jax.numpy as jnp
from jax import lax
from jax.sharding import PartitionSpec as P

TILE = 128
NSUB = 4
HIGHEST = lax.Precision.HIGHEST


def passed_along(value, axis, steps):
    count = lax.axis_size(axis)
    initial, last = (max(0, -steps), min(count, count - steps))
    return lax.ppermute(value, axis, [(source, source + steps) for source in range(initial, last)])


def from_behind(array, axis, by):
    count = lax.axis_size(axis)
    return lax.ppermute(array, axis, [(i, (i + by) % count) for i in range(count)])


def wide_halo(array, width):
    south = passed_along(array[..., -8:, :], "col", 1)[..., -width:, :]
    north = passed_along(array[..., :8, :], "col", -1)[..., :width, :]
    array = jnp.concatenate([south, array, north], axis=-2)
    west = from_behind(array[..., -TILE:], "panel", 1)[..., -width:]
    east = from_behind(array[..., :TILE], "panel", -1)[..., :width]
    return jnp.concatenate([west, array, east], axis=-1)


def vertical_mix(tracer, mixing):
    level_flux = mixing[:-1] * (tracer[:, 1:] - tracer[:, :-1])
    zero_level = jnp.zeros_like(tracer[:, :1])
    from_above = jnp.concatenate([level_flux, zero_level], axis=1)
    from_below = jnp.concatenate([zero_level, level_flux], axis=1)
    relaxation = jnp.concatenate(
        [jnp.zeros_like(tracer[:, :-1]), mixing[-1:] * tracer[:, -1:]], axis=1
    )
    return tracer + from_above - from_below - relaxation


def advect_mix(tracer, east_vel, north_vel, mixing):
    centre = tracer[..., 1:-1, 1:-1]
    vel_east = east_vel[:, 1:-1, 1:-1]
    vel_west = east_vel[:, 1:-1, :-2]
    vel_north = north_vel[:, 1:-1, 1:-1]
    vel_south = north_vel[:, :-2, 1:-1]
    flux_east = (
        jnp.maximum(vel_east, 0.0) * centre + jnp.minimum(vel_east, 0.0) * tracer[..., 1:-1, 2:]
    )
    flux_west = (
        jnp.maximum(vel_west, 0.0) * tracer[..., 1:-1, :-2] + jnp.minimum(vel_west, 0.0) * centre
    )
    flux_north = (
        jnp.maximum(vel_north, 0.0) * centre + jnp.minimum(vel_north, 0.0) * tracer[..., 2:, 1:-1]
    )
    flux_south = (
        jnp.maximum(vel_south, 0.0) * tracer[..., :-2, 1:-1] + jnp.minimum(vel_south, 0.0) * centre
    )
    advanced = centre - (flux_east - flux_west) - (flux_north - flux_south)
    return vertical_mix(advanced, mixing[:, 1:-1, 1:-1])


def to_tiles(field_grid):
    fcount, grid_rows, grid_cols = field_grid.shape
    blocks = field_grid.reshape(fcount, grid_rows, grid_cols // TILE, TILE)
    return blocks.transpose(1, 2, 0, 3).reshape(-1, fcount, TILE)


def from_tiles(tile_form, grid_rows, grid_cols):
    fcount = tile_form.shape[1]
    blocks = tile_form.reshape(grid_rows, grid_cols // TILE, fcount, TILE)
    return blocks.transpose(2, 0, 1, 3).reshape(fcount, grid_rows, grid_cols)


def bucket_places(partner_devices, owners, capacity):
    owner_list = partner_devices.reshape(-1)
    owner_hit = (owner_list[:, None] == jnp.arange(owners, dtype=jnp.int32)[None, :]).astype(
        jnp.int32
    )
    owner_rank = jnp.cumsum(owner_hit, axis=0) - owner_hit
    position = jnp.sum(owner_rank * owner_hit, axis=1)
    return owner_list * capacity + position


def advect(start, coeffs, grid_rows):
    fields = start.shape[0] * start.shape[1]
    both = jnp.concatenate([start.reshape((fields,) + start.shape[2:]), coeffs.reshape((-1,) + coeffs.shape[2:])])
    wide = wide_halo(both, NSUB)
    levels = coeffs.shape[1]
    tracer = wide[:fields].reshape(start.shape[:2] + wide.shape[1:])
    coeff_ext = wide[fields:].reshape((3, levels) + wide.shape[1:])
    rows_total = grid_rows * lax.axis_size("col")
    row_global = (
        lax.axis_index("col") * grid_rows
        + jnp.arange(grid_rows + 2 * NSUB, dtype=jnp.int32)
        - NSUB
    )
    row_open = ((row_global >= 0) & (row_global < rows_total - 1)).astype(jnp.float32)
    east_ext = coeff_ext[0]
    north_ext = coeff_ext[1] * row_open[None, :, None]
    mix_ext = coeff_ext[2]
    for step_index in range(NSUB):
        s = step_index
        e = east_ext.shape[1] - s
        w = east_ext.shape[2] - s
        tracer = advect_mix(
            tracer,
            east_ext[:, s:e, s:w],
            north_ext[:, s:e, s:w],
            mix_ext[:, s:e, s:w],
        )
    return tracer


def on_device(
    joint_tracer_field,
    courant_mixing_rates,
    oceanic_indicator,
    glacial_indicator,
    prior_oceanic_warmth,
    prior_glacial_cover,
    partner_devices,
    receiving_tile_index,
    bank_tile_entry,
    conservative_overlay_factors,
):
    owners = lax.axis_size("panel") * lax.axis_size("col")
    tile_count = partner_devices.shape[0]
    capacity = max(2, 4 * tile_count // owners)
    slots = owners * capacity
    nbank = conservative_overlay_factors.shape[0]
    on_atmos = lax.axis_index("comp") == 0
    device_tracer_share = joint_tracer_field[0]
    coeffs = courant_mixing_rates[0]
    grid_rows = coeffs.shape[2]
    grid_cols = coeffs.shape[3]
    sea_here = oceanic_indicator[0].astype(jnp.float32)
    wind_east = coeffs[0, 0]
    wind_north = coeffs[1, 0]
    airflow_speed = jnp.sqrt(wind_east * wind_east + wind_north * wind_north + 0.01)
    unfrozen_share = sea_here * (1.0 - prior_glacial_cover)
    thermal_exchange_rate = (
        2.0 * airflow_speed * (prior_oceanic_warmth - device_tracer_share[0, 0]) * unfrozen_share
    )
    evaporation_rate = (
        2.0
        * airflow_speed
        * (jnp.exp(0.1 * prior_oceanic_warmth) - device_tracer_share[1, 0])
        * unfrozen_share
    )
    start = jnp.concatenate(
        [
            (device_tracer_share[0, 0] + jnp.where(on_atmos, thermal_exchange_rate, 0.0))[None],
            device_tracer_share[0, 1:],
            (device_tracer_share[1, 0] + jnp.where(on_atmos, evaporation_rate, 0.0))[None],
            device_tracer_share[1, 1:],
        ]
    ).reshape(device_tracer_share.shape)
    surface_flux = jnp.stack([thermal_exchange_rate, evaporation_rate])
    flux_rows = passed_along(to_tiles(surface_flux), "comp", 1).reshape(tile_count * 2, TILE)
    pairs = tile_count * 2

    bucket_place = bucket_places(partner_devices, owners, capacity)
    place_match = bucket_place[None, :] == jnp.arange(slots, dtype=jnp.int32)[:, None]
    slot_used = jnp.any(place_match, axis=1)
    slot_pair = jnp.sum(jnp.where(place_match, jnp.arange(pairs, dtype=jnp.int32)[None, :], 0), axis=1)
    slot_tile = slot_pair // 2
    slot_bank = jnp.sum(jnp.where(place_match, bank_tile_entry.reshape(-1)[None, :], 0), axis=1)

    by_bank = jnp.einsum(
        "bji,ri->brj", conservative_overlay_factors, flux_rows, precision=lax.Precision.HIGH
    ).reshape(nbank * pairs, TILE)
    f_ids = jnp.arange(2, dtype=jnp.int32)[None, :]
    slot_rows = (slot_bank * pairs + slot_tile * 2)[:, None] + f_ids
    picked = by_bank[slot_rows.reshape(-1)].reshape(slots, 2, TILE)
    buffer = jnp.where(slot_used[:, None, None], picked, 0.0).reshape(owners, capacity * 2, TILE)
    slot_label = jnp.sum(jnp.where(place_match, receiving_tile_index.reshape(-1)[None, :], 0), axis=1)
    label_row = jnp.pad(
        slot_label.reshape(owners, capacity).astype(jnp.float32), ((0, 0), (0, TILE - capacity))
    )
    bucket = jnp.concatenate([buffer, label_row[:, None, :]], axis=1)
    rows_out = capacity * 2 + 1
    arrived = lax.all_to_all(
        bucket.reshape(owners, rows_out * TILE), ("panel", "col"), 0, 0, tiled=True
    ).reshape(owners, rows_out, TILE)
    received = arrived[:, : capacity * 2].reshape(slots * 2, TILE)
    recv_slots = arrived[:, capacity * 2, :capacity].astype(jnp.int32).reshape(-1)

    row_ids = lax.broadcasted_iota(jnp.int32, (pairs, slots * 2), 0)
    col_ids = lax.broadcasted_iota(jnp.int32, (pairs, slots * 2), 1)
    recv_rep = jnp.broadcast_to(recv_slots[:, None], (slots, 2)).reshape(-1)
    slot_hit2 = (
        (recv_rep[None, :] == row_ids // 2) & (col_ids % 2 == row_ids % 2)
    ).astype(jnp.float32)
    summed = jnp.dot(slot_hit2, received, precision=HIGHEST)
    forcing = from_tiles(summed.reshape(tile_count, 2, TILE), grid_rows, grid_cols)

    tracer = advect(start, coeffs, grid_rows)
    forced = (
        tracer.at[0, 0]
        .add(-(0.5 * sea_here * forcing[0]))
        .at[1, 0]
        .add(0.5 * sea_here * forcing[1])
    )
    new_here = jnp.where(on_atmos, tracer, forced)
    sea_temp = new_here[0, 0]
    ice_cover = (
        glacial_indicator.astype(jnp.float32) * sea_here * jnp.clip(0.5 - sea_temp, 0.0, 1.0)
    )
    ocean_surface = jnp.stack([sea_temp, ice_cover])
    ocean_tiles = to_tiles(ocean_surface).reshape(pairs, TILE)
    reply = jnp.dot(slot_hit2.T, ocean_tiles, precision=HIGHEST).reshape(owners, capacity * 2, TILE)
    returned = lax.all_to_all(reply, ("panel", "col"), 0, 0, tiled=True).reshape(slots * 2, TILE)
    place_rep = jnp.broadcast_to(bucket_place[:, None], (pairs, 2)).reshape(-1)
    p_rows = lax.broadcasted_iota(jnp.int32, (pairs * 2, slots * 2), 0)
    p_cols = lax.broadcasted_iota(jnp.int32, (pairs * 2, slots * 2), 1)
    place_hit2 = ((place_rep[:, None] == p_cols // 2) & (p_cols % 2 == p_rows % 2)).astype(
        jnp.float32
    )
    values = jnp.dot(place_hit2, returned, precision=HIGHEST)

    by_bank_back = jnp.einsum(
        "rj,bji->bri", values, conservative_overlay_factors, precision=lax.Precision.HIGH
    ).reshape(nbank * pairs * 2, TILE)
    tile_ids = jnp.arange(tile_count, dtype=jnp.int32)[:, None]
    pair_rows = (bank_tile_entry * tile_count + tile_ids) * 4 + jnp.arange(2, dtype=jnp.int32)[None, :] * 2
    back_rows = pair_rows[:, :, None] + f_ids[:, None, :]
    numerator = jnp.sum(by_bank_back[back_rows.reshape(-1)].reshape(tile_count, 2, 2, TILE), axis=1)
    column_sums = jnp.sum(conservative_overlay_factors, axis=1)
    bank_ids = jnp.arange(nbank, dtype=jnp.int32)[None, :]
    bank_count = (bank_tile_entry[:, :1] == bank_ids).astype(jnp.float32) + (
        bank_tile_entry[:, 1:] == bank_ids
    ).astype(jnp.float32)
    denominator = jnp.dot(bank_count, column_sums, precision=HIGHEST)
    remap_back = numerator / denominator[:, None, :]
    remapped = passed_along(from_tiles(remap_back, grid_rows, grid_cols), "comp", -1)
    surface_here = jnp.where(on_atmos, remapped, ocean_surface)
    return (new_here[None], surface_here[None])


def solution(mesh):
    return jax.shard_map(
        on_device,
        mesh=mesh,
        in_specs=(
            P("comp", None, None, "col", "panel"),
            P("comp", None, None, "col", "panel"),
            P("comp", "col", "panel"),
            P("col", "panel"),
            P("col", "panel"),
            P("col", "panel"),
            P(("panel", "col"), None),
            P(("panel", "col"), None),
            P(("panel", "col"), None),
            P(),
        ),
        out_specs=(P("comp", None, None, "col", "panel"), P("comp", None, "col", "panel")),
        check_vma=False,
    )
```

```python
import jax
import jax.numpy as jnp
from jax import lax
from jax.sharding import PartitionSpec as P

TILE = 128
NSUB = 4
HIGHEST = lax.Precision.HIGHEST


def passed_along(value, axis, steps):
    count = lax.axis_size(axis)
    initial, last = (max(0, -steps), min(count, count - steps))
    return lax.ppermute(value, axis, [(source, source + steps) for source in range(initial, last)])


def from_behind(array, axis, by):
    count = lax.axis_size(axis)
    return lax.ppermute(array, axis, [(i, (i + by) % count) for i in range(count)])


def wide_halo(array, width):
    south = passed_along(array[..., -8:, :], "col", 1)[..., -width:, :]
    north = passed_along(array[..., :8, :], "col", -1)[..., :width, :]
    array = jnp.concatenate([south, array, north], axis=-2)
    west = from_behind(array[..., -TILE:], "panel", 1)[..., -width:]
    east = from_behind(array[..., :TILE], "panel", -1)[..., :width]
    return jnp.concatenate([west, array, east], axis=-1)


def vertical_mix(tracer, mixing):
    level_flux = mixing[:-1] * (tracer[:, 1:] - tracer[:, :-1])
    zero_level = jnp.zeros_like(tracer[:, :1])
    from_above = jnp.concatenate([level_flux, zero_level], axis=1)
    from_below = jnp.concatenate([zero_level, level_flux], axis=1)
    relaxation = jnp.concatenate(
        [jnp.zeros_like(tracer[:, :-1]), mixing[-1:] * tracer[:, -1:]], axis=1
    )
    return tracer + from_above - from_below - relaxation


def advect_mix(tracer, east_vel, north_vel, mixing):
    centre = tracer[..., 1:-1, 1:-1]
    vel_east = east_vel[:, 1:-1, 1:-1]
    vel_west = east_vel[:, 1:-1, :-2]
    vel_north = north_vel[:, 1:-1, 1:-1]
    vel_south = north_vel[:, :-2, 1:-1]
    flux_east = (
        jnp.maximum(vel_east, 0.0) * centre + jnp.minimum(vel_east, 0.0) * tracer[..., 1:-1, 2:]
    )
    flux_west = (
        jnp.maximum(vel_west, 0.0) * tracer[..., 1:-1, :-2] + jnp.minimum(vel_west, 0.0) * centre
    )
    flux_north = (
        jnp.maximum(vel_north, 0.0) * centre + jnp.minimum(vel_north, 0.0) * tracer[..., 2:, 1:-1]
    )
    flux_south = (
        jnp.maximum(vel_south, 0.0) * tracer[..., :-2, 1:-1] + jnp.minimum(vel_south, 0.0) * centre
    )
    advanced = centre - (flux_east - flux_west) - (flux_north - flux_south)
    return vertical_mix(advanced, mixing[:, 1:-1, 1:-1])


def to_tiles(field_grid):
    fcount, grid_rows, grid_cols = field_grid.shape
    blocks = field_grid.reshape(fcount, grid_rows, grid_cols // TILE, TILE)
    return blocks.transpose(1, 2, 0, 3).reshape(-1, fcount, TILE)


def from_tiles(tile_form, grid_rows, grid_cols):
    fcount = tile_form.shape[1]
    blocks = tile_form.reshape(grid_rows, grid_cols // TILE, fcount, TILE)
    return blocks.transpose(2, 0, 1, 3).reshape(fcount, grid_rows, grid_cols)


def bucket_places(partner_devices, owners, capacity):
    owner_list = partner_devices.reshape(-1)
    owner_hit = (owner_list[:, None] == jnp.arange(owners, dtype=jnp.int32)[None, :]).astype(
        jnp.int32
    )
    owner_rank = jnp.cumsum(owner_hit, axis=0) - owner_hit
    position = jnp.sum(owner_rank * owner_hit, axis=1)
    return owner_list * capacity + position


def advect(start, coeffs, grid_rows):
    fields = start.shape[0] * start.shape[1]
    both = jnp.concatenate([start.reshape((fields,) + start.shape[2:]), coeffs.reshape((-1,) + coeffs.shape[2:])])
    wide = wide_halo(both, NSUB)
    levels = coeffs.shape[1]
    tracer = wide[:fields].reshape(start.shape[:2] + wide.shape[1:])
    coeff_ext = wide[fields:].reshape((3, levels) + wide.shape[1:])
    rows_total = grid_rows * lax.axis_size("col")
    row_global = (
        lax.axis_index("col") * grid_rows
        + jnp.arange(grid_rows + 2 * NSUB, dtype=jnp.int32)
        - NSUB
    )
    row_open = ((row_global >= 0) & (row_global < rows_total - 1)).astype(jnp.float32)
    east_ext = coeff_ext[0]
    north_ext = coeff_ext[1] * row_open[None, :, None]
    mix_ext = coeff_ext[2]
    for step_index in range(NSUB):
        s = step_index
        e = east_ext.shape[1] - s
        w = east_ext.shape[2] - s
        tracer = advect_mix(
            tracer,
            east_ext[:, s:e, s:w],
            north_ext[:, s:e, s:w],
            mix_ext[:, s:e, s:w],
        )
    return tracer


def on_device(
    joint_tracer_field,
    courant_mixing_rates,
    oceanic_indicator,
    glacial_indicator,
    prior_oceanic_warmth,
    prior_glacial_cover,
    partner_devices,
    receiving_tile_index,
    bank_tile_entry,
    conservative_overlay_factors,
):
    owners = lax.axis_size("panel") * lax.axis_size("col")
    tile_count = partner_devices.shape[0]
    capacity = max(2, 4 * tile_count // owners)
    slots = owners * capacity
    nbank = conservative_overlay_factors.shape[0]
    on_atmos = lax.axis_index("comp") == 0
    device_tracer_share = joint_tracer_field[0]
    coeffs = courant_mixing_rates[0]
    grid_rows = coeffs.shape[2]
    grid_cols = coeffs.shape[3]
    sea_here = oceanic_indicator[0].astype(jnp.float32)
    wind_east = coeffs[0, 0]
    wind_north = coeffs[1, 0]
    airflow_speed = jnp.sqrt(wind_east * wind_east + wind_north * wind_north + 0.01)
    unfrozen_share = sea_here * (1.0 - prior_glacial_cover)
    thermal_exchange_rate = (
        2.0 * airflow_speed * (prior_oceanic_warmth - device_tracer_share[0, 0]) * unfrozen_share
    )
    evaporation_rate = (
        2.0
        * airflow_speed
        * (jnp.exp(0.1 * prior_oceanic_warmth) - device_tracer_share[1, 0])
        * unfrozen_share
    )
    heated = device_tracer_share.at[0, 0].add(thermal_exchange_rate).at[1, 0].add(evaporation_rate)
    start = jnp.where(on_atmos, heated, device_tracer_share)
    surface_flux = jnp.stack([thermal_exchange_rate, evaporation_rate])
    flux_rows = passed_along(to_tiles(surface_flux), "comp", 1).reshape(tile_count * 2, TILE)
    pairs = tile_count * 2

    bucket_place = bucket_places(partner_devices, owners, capacity)
    place_match = bucket_place[None, :] == jnp.arange(slots, dtype=jnp.int32)[:, None]
    slot_used = jnp.any(place_match, axis=1)
    slot_pair = jnp.sum(jnp.where(place_match, jnp.arange(pairs, dtype=jnp.int32)[None, :], 0), axis=1)
    slot_tile = slot_pair // 2
    slot_bank = jnp.sum(jnp.where(place_match, bank_tile_entry.reshape(-1)[None, :], 0), axis=1)

    by_bank = jnp.einsum(
        "bji,ri->brj", conservative_overlay_factors, flux_rows, precision=lax.Precision.HIGH
    ).reshape(nbank * pairs, TILE)
    f_ids = jnp.arange(2, dtype=jnp.int32)[None, :]
    slot_rows = (slot_bank * pairs + slot_tile * 2)[:, None] + f_ids
    picked = by_bank[slot_rows.reshape(-1)].reshape(slots, 2, TILE)
    buffer = jnp.where(slot_used[:, None, None], picked, 0.0).reshape(owners, capacity * 2, TILE)
    slot_label = jnp.sum(jnp.where(place_match, receiving_tile_index.reshape(-1)[None, :], 0), axis=1)
    label_row = jnp.pad(
        slot_label.reshape(owners, capacity).astype(jnp.float32), ((0, 0), (0, TILE - capacity))
    )
    bucket = jnp.concatenate([buffer, label_row[:, None, :]], axis=1)
    rows_out = capacity * 2 + 1
    arrived = lax.all_to_all(
        bucket.reshape(owners, rows_out * TILE), ("panel", "col"), 0, 0, tiled=True
    ).reshape(owners, rows_out, TILE)
    received = arrived[:, : capacity * 2].reshape(slots * 2, TILE)
    recv_slots = arrived[:, capacity * 2, :capacity].astype(jnp.int32).reshape(-1)

    row_ids = lax.broadcasted_iota(jnp.int32, (pairs, slots * 2), 0)
    col_ids = lax.broadcasted_iota(jnp.int32, (pairs, slots * 2), 1)
    recv_rep = jnp.broadcast_to(recv_slots[:, None], (slots, 2)).reshape(-1)
    slot_hit2 = (
        (recv_rep[None, :] == row_ids // 2) & (col_ids % 2 == row_ids % 2)
    ).astype(jnp.float32)
    summed = jnp.dot(slot_hit2, received, precision=HIGHEST)
    forcing = from_tiles(summed.reshape(tile_count, 2, TILE), grid_rows, grid_cols)

    tracer = advect(start, coeffs, grid_rows)
    forced = (
        tracer.at[0, 0]
        .add(-(0.5 * sea_here * forcing[0]))
        .at[1, 0]
        .add(0.5 * sea_here * forcing[1])
    )
    new_here = jnp.where(on_atmos, tracer, forced)
    sea_temp = new_here[0, 0]
    ice_cover = (
        glacial_indicator.astype(jnp.float32) * sea_here * jnp.clip(0.5 - sea_temp, 0.0, 1.0)
    )
    ocean_surface = jnp.stack([sea_temp, ice_cover])
    ocean_tiles = to_tiles(ocean_surface).reshape(pairs, TILE)
    reply = jnp.dot(slot_hit2.T, ocean_tiles, precision=HIGHEST).reshape(owners, capacity * 2, TILE)
    returned = lax.all_to_all(reply, ("panel", "col"), 0, 0, tiled=True).reshape(slots * 2, TILE)
    reply, late_place = lax.optimization_barrier((reply, bucket_place))
    place_rep = jnp.broadcast_to(late_place[:, None], (pairs, 2)).reshape(-1)
    p_rows = lax.broadcasted_iota(jnp.int32, (pairs * 2, slots * 2), 0)
    p_cols = lax.broadcasted_iota(jnp.int32, (pairs * 2, slots * 2), 1)
    place_hit2 = ((place_rep[:, None] == p_cols // 2) & (p_cols % 2 == p_rows % 2)).astype(
        jnp.float32
    )
    values = jnp.dot(place_hit2, returned, precision=HIGHEST)

    by_bank_back = jnp.einsum(
        "rj,bji->bri", values, conservative_overlay_factors, precision=lax.Precision.HIGH
    ).reshape(nbank * pairs * 2, TILE)
    tile_ids = jnp.arange(tile_count, dtype=jnp.int32)[:, None]
    pair_rows = (bank_tile_entry * tile_count + tile_ids) * 4 + jnp.arange(2, dtype=jnp.int32)[None, :] * 2
    back_rows = pair_rows[:, :, None] + f_ids[:, None, :]
    numerator = jnp.sum(by_bank_back[back_rows.reshape(-1)].reshape(tile_count, 2, 2, TILE), axis=1)
    column_sums = jnp.sum(conservative_overlay_factors, axis=1)
    bank_ids = jnp.arange(nbank, dtype=jnp.int32)[None, :]
    bank_count = (bank_tile_entry[:, :1] == bank_ids).astype(jnp.float32) + (
        bank_tile_entry[:, 1:] == bank_ids
    ).astype(jnp.float32)
    denominator = jnp.dot(bank_count, column_sums, precision=HIGHEST)
    remap_back = numerator / denominator[:, None, :]
    remapped = passed_along(from_tiles(remap_back, grid_rows, grid_cols), "comp", -1)
    surface_here = jnp.where(on_atmos, remapped, ocean_surface)
    return (new_here[None], surface_here[None])


def solution(mesh):
    return jax.shard_map(
        on_device,
        mesh=mesh,
        in_specs=(
            P("comp", None, None, "col", "panel"),
            P("comp", None, None, "col", "panel"),
            P("comp", "col", "panel"),
            P("col", "panel"),
            P("col", "panel"),
            P("col", "panel"),
            P(("panel", "col"), None),
            P(("panel", "col"), None),
            P(("panel", "col"), None),
            P(),
        ),
        out_specs=(P("comp", None, None, "col", "panel"), P("comp", None, "col", "panel")),
        check_vma=False,
    )
```

```python
import jax
import jax.numpy as jnp
from jax import lax
from jax.sharding import PartitionSpec as P

TILE = 128
NSUB = 4
HIGHEST = lax.Precision.HIGHEST


def passed_along(value, axis, steps):
    count = lax.axis_size(axis)
    initial, last = (max(0, -steps), min(count, count - steps))
    return lax.ppermute(value, axis, [(source, source + steps) for source in range(initial, last)])


def from_behind(array, axis, by):
    count = lax.axis_size(axis)
    return lax.ppermute(array, axis, [(i, (i + by) % count) for i in range(count)])


def wide_halo(array, width):
    south = passed_along(array[..., -8:, :], "col", 1)[..., -width:, :]
    north = passed_along(array[..., :8, :], "col", -1)[..., :width, :]
    array = jnp.concatenate([south, array, north], axis=-2)
    west = from_behind(array[..., -TILE:], "panel", 1)[..., -width:]
    east = from_behind(array[..., :TILE], "panel", -1)[..., :width]
    return jnp.concatenate([west, array, east], axis=-1)


def vertical_mix(tracer, mixing):
    level_flux = mixing[:-1] * (tracer[:, 1:] - tracer[:, :-1])
    zero_level = jnp.zeros_like(tracer[:, :1])
    from_above = jnp.concatenate([level_flux, zero_level], axis=1)
    from_below = jnp.concatenate([zero_level, level_flux], axis=1)
    relaxation = jnp.concatenate(
        [jnp.zeros_like(tracer[:, :-1]), mixing[-1:] * tracer[:, -1:]], axis=1
    )
    return tracer + from_above - from_below - relaxation


def advect_mix(tracer, east_vel, north_vel, mixing):
    centre = tracer[..., 1:-1, 1:-1]
    vel_east = east_vel[:, 1:-1, 1:-1]
    vel_west = east_vel[:, 1:-1, :-2]
    vel_north = north_vel[:, 1:-1, 1:-1]
    vel_south = north_vel[:, :-2, 1:-1]
    flux_east = (
        jnp.maximum(vel_east, 0.0) * centre + jnp.minimum(vel_east, 0.0) * tracer[..., 1:-1, 2:]
    )
    flux_west = (
        jnp.maximum(vel_west, 0.0) * tracer[..., 1:-1, :-2] + jnp.minimum(vel_west, 0.0) * centre
    )
    flux_north = (
        jnp.maximum(vel_north, 0.0) * centre + jnp.minimum(vel_north, 0.0) * tracer[..., 2:, 1:-1]
    )
    flux_south = (
        jnp.maximum(vel_south, 0.0) * tracer[..., :-2, 1:-1] + jnp.minimum(vel_south, 0.0) * centre
    )
    advanced = centre - (flux_east - flux_west) - (flux_north - flux_south)
    return vertical_mix(advanced, mixing[:, 1:-1, 1:-1])


def to_tiles(field_grid):
    fcount, grid_rows, grid_cols = field_grid.shape
    blocks = field_grid.reshape(fcount, grid_rows, grid_cols // TILE, TILE)
    return blocks.transpose(1, 2, 0, 3).reshape(-1, fcount, TILE)


def from_tiles(tile_form, grid_rows, grid_cols):
    fcount = tile_form.shape[1]
    blocks = tile_form.reshape(grid_rows, grid_cols // TILE, fcount, TILE)
    return blocks.transpose(2, 0, 1, 3).reshape(fcount, grid_rows, grid_cols)


def bucket_places(partner_devices, owners, capacity):
    owner_list = partner_devices.reshape(-1)
    owner_hit = (owner_list[:, None] == jnp.arange(owners, dtype=jnp.int32)[None, :]).astype(
        jnp.int32
    )
    owner_rank = jnp.cumsum(owner_hit, axis=0) - owner_hit
    position = jnp.sum(owner_rank * owner_hit, axis=1)
    return owner_list * capacity + position


def advect(start, coeffs, grid_rows):
    fields = start.shape[0] * start.shape[1]
    both = jnp.concatenate([start.reshape((fields,) + start.shape[2:]), coeffs.reshape((-1,) + coeffs.shape[2:])])
    wide = wide_halo(both, NSUB)
    levels = coeffs.shape[1]
    tracer = wide[:fields].reshape(start.shape[:2] + wide.shape[1:])
    coeff_ext = wide[fields:].reshape((3, levels) + wide.shape[1:])
    rows_total = grid_rows * lax.axis_size("col")
    row_global = (
        lax.axis_index("col") * grid_rows
        + jnp.arange(grid_rows + 2 * NSUB, dtype=jnp.int32)
        - NSUB
    )
    row_open = ((row_global >= 0) & (row_global < rows_total - 1)).astype(jnp.float32)
    east_ext = coeff_ext[0]
    north_ext = coeff_ext[1] * row_open[None, :, None]
    mix_ext = coeff_ext[2]
    for step_index in range(NSUB):
        s = step_index
        e = east_ext.shape[1] - s
        w = east_ext.shape[2] - s
        tracer = advect_mix(
            tracer,
            east_ext[:, s:e, s:w],
            north_ext[:, s:e, s:w],
            mix_ext[:, s:e, s:w],
        )
    return tracer


def on_device(
    joint_tracer_field,
    courant_mixing_rates,
    oceanic_indicator,
    glacial_indicator,
    prior_oceanic_warmth,
    prior_glacial_cover,
    partner_devices,
    receiving_tile_index,
    bank_tile_entry,
    conservative_overlay_factors,
):
    owners = lax.axis_size("panel") * lax.axis_size("col")
    tile_count = partner_devices.shape[0]
    capacity = max(2, 4 * tile_count // owners)
    slots = owners * capacity
    nbank = conservative_overlay_factors.shape[0]
    on_atmos = lax.axis_index("comp") == 0
    device_tracer_share = joint_tracer_field[0]
    coeffs = courant_mixing_rates[0]
    grid_rows = coeffs.shape[2]
    grid_cols = coeffs.shape[3]
    sea_here = oceanic_indicator[0].astype(jnp.float32)
    wind_east = coeffs[0, 0]
    wind_north = coeffs[1, 0]
    airflow_speed = jnp.sqrt(wind_east * wind_east + wind_north * wind_north + 0.01)
    unfrozen_share = sea_here * (1.0 - prior_glacial_cover)
    thermal_exchange_rate = (
        2.0 * airflow_speed * (prior_oceanic_warmth - device_tracer_share[0, 0]) * unfrozen_share
    )
    evaporation_rate = (
        2.0
        * airflow_speed
        * (jnp.exp(0.1 * prior_oceanic_warmth) - device_tracer_share[1, 0])
        * unfrozen_share
    )
    heated = device_tracer_share.at[0, 0].add(thermal_exchange_rate).at[1, 0].add(evaporation_rate)
    start = jnp.where(on_atmos, heated, device_tracer_share)
    surface_flux = jnp.stack([thermal_exchange_rate, evaporation_rate])
    flux_rows = passed_along(to_tiles(surface_flux), "comp", 1).reshape(tile_count * 2, TILE)
    pairs = tile_count * 2

    bucket_place = bucket_places(partner_devices, owners, capacity)
    place_match = bucket_place[None, :] == jnp.arange(slots, dtype=jnp.int32)[:, None]
    slot_used = jnp.any(place_match, axis=1)
    slot_pair = jnp.sum(jnp.where(place_match, jnp.arange(pairs, dtype=jnp.int32)[None, :], 0), axis=1)
    slot_tile = slot_pair // 2
    slot_bank = jnp.sum(jnp.where(place_match, bank_tile_entry.reshape(-1)[None, :], 0), axis=1)

    by_bank = jnp.einsum(
        "bji,ri->brj", conservative_overlay_factors, flux_rows, precision=lax.Precision.HIGH
    ).reshape(nbank * pairs, TILE)
    f_ids = jnp.arange(2, dtype=jnp.int32)[None, :]
    slot_rows = (slot_bank * pairs + slot_tile * 2)[:, None] + f_ids
    picked = by_bank[slot_rows.reshape(-1)].reshape(slots, 2, TILE)
    buffer = jnp.where(slot_used[:, None, None], picked, 0.0).reshape(owners, capacity * 2, TILE)
    slot_label = jnp.sum(jnp.where(place_match, receiving_tile_index.reshape(-1)[None, :], 0), axis=1)
    label_row = jnp.pad(
        slot_label.reshape(owners, capacity).astype(jnp.float32), ((0, 0), (0, TILE - capacity))
    )
    bucket = jnp.concatenate([buffer, label_row[:, None, :]], axis=1)
    rows_out = capacity * 2 + 1
    arrived = lax.all_to_all(
        bucket.reshape(owners, rows_out * TILE), ("panel", "col"), 0, 0, tiled=True
    ).reshape(owners, rows_out, TILE)
    received = arrived[:, : capacity * 2].reshape(slots * 2, TILE)
    recv_slots = arrived[:, capacity * 2, :capacity].astype(jnp.int32).reshape(-1)

    row_ids = lax.broadcasted_iota(jnp.int32, (pairs, slots * 2), 0)
    col_ids = lax.broadcasted_iota(jnp.int32, (pairs, slots * 2), 1)
    recv_rep = jnp.broadcast_to(recv_slots[:, None], (slots, 2)).reshape(-1)
    slot_hit2 = (
        (recv_rep[None, :] == row_ids // 2) & (col_ids % 2 == row_ids % 2)
    ).astype(jnp.float32)
    summed = jnp.dot(slot_hit2, received, precision=lax.Precision.HIGH)
    forcing = from_tiles(summed.reshape(tile_count, 2, TILE), grid_rows, grid_cols)

    tracer = advect(start, coeffs, grid_rows)
    forced = (
        tracer.at[0, 0]
        .add(-(0.5 * sea_here * forcing[0]))
        .at[1, 0]
        .add(0.5 * sea_here * forcing[1])
    )
    new_here = jnp.where(on_atmos, tracer, forced)
    sea_temp = new_here[0, 0]
    ice_cover = (
        glacial_indicator.astype(jnp.float32) * sea_here * jnp.clip(0.5 - sea_temp, 0.0, 1.0)
    )
    ocean_surface = jnp.stack([sea_temp, ice_cover])
    ocean_tiles = to_tiles(ocean_surface).reshape(pairs, TILE)
    reply = jnp.dot(slot_hit2.T, ocean_tiles, precision=lax.Precision.HIGH).reshape(owners, capacity * 2, TILE)
    returned = lax.all_to_all(reply, ("panel", "col"), 0, 0, tiled=True).reshape(slots * 2, TILE)
    place_rep = jnp.broadcast_to(bucket_place[:, None], (pairs, 2)).reshape(-1)
    p_rows = lax.broadcasted_iota(jnp.int32, (pairs * 2, slots * 2), 0)
    p_cols = lax.broadcasted_iota(jnp.int32, (pairs * 2, slots * 2), 1)
    place_hit2 = ((place_rep[:, None] == p_cols // 2) & (p_cols % 2 == p_rows % 2)).astype(
        jnp.float32
    )
    values = jnp.dot(place_hit2, returned, precision=lax.Precision.HIGH)

    by_bank_back = jnp.einsum(
        "rj,bji->bri", values, conservative_overlay_factors, precision=lax.Precision.HIGH
    ).reshape(nbank * pairs * 2, TILE)
    tile_ids = jnp.arange(tile_count, dtype=jnp.int32)[:, None]
    pair_rows = (bank_tile_entry * tile_count + tile_ids) * 4 + jnp.arange(2, dtype=jnp.int32)[None, :] * 2
    back_rows = pair_rows[:, :, None] + f_ids[:, None, :]
    numerator = jnp.sum(by_bank_back[back_rows.reshape(-1)].reshape(tile_count, 2, 2, TILE), axis=1)
    column_sums = jnp.sum(conservative_overlay_factors, axis=1)
    bank_ids = jnp.arange(nbank, dtype=jnp.int32)[None, :]
    bank_count = (bank_tile_entry[:, :1] == bank_ids).astype(jnp.float32) + (
        bank_tile_entry[:, 1:] == bank_ids
    ).astype(jnp.float32)
    denominator = jnp.dot(bank_count, column_sums, precision=lax.Precision.HIGH)
    remap_back = numerator / denominator[:, None, :]
    remapped = passed_along(from_tiles(remap_back, grid_rows, grid_cols), "comp", -1)
    surface_here = jnp.where(on_atmos, remapped, ocean_surface)
    return (new_here[None], surface_here[None])


def solution(mesh):
    return jax.shard_map(
        on_device,
        mesh=mesh,
        in_specs=(
            P("comp", None, None, "col", "panel"),
            P("comp", None, None, "col", "panel"),
            P("comp", "col", "panel"),
            P("col", "panel"),
            P("col", "panel"),
            P("col", "panel"),
            P(("panel", "col"), None),
            P(("panel", "col"), None),
            P(("panel", "col"), None),
            P(),
        ),
        out_specs=(P("comp", None, None, "col", "panel"), P("comp", None, "col", "panel")),
        check_vma=False,
    )
```

```python
import jax
import jax.numpy as jnp
from jax import lax
from jax.sharding import PartitionSpec as P

TILE = 128
NSUB = 4
HIGHEST = lax.Precision.HIGHEST


def passed_along(value, axis, steps):
    count = lax.axis_size(axis)
    initial, last = (max(0, -steps), min(count, count - steps))
    return lax.ppermute(value, axis, [(source, source + steps) for source in range(initial, last)])


def from_behind(array, axis, by):
    count = lax.axis_size(axis)
    return lax.ppermute(array, axis, [(i, (i + by) % count) for i in range(count)])


def wide_halo(array, width):
    south = passed_along(array[..., -8:, :], "col", 1)[..., -width:, :]
    north = passed_along(array[..., :8, :], "col", -1)[..., :width, :]
    array = jnp.concatenate([south, array, north], axis=-2)
    west = from_behind(array[..., -TILE:], "panel", 1)[..., -width:]
    east = from_behind(array[..., :TILE], "panel", -1)[..., :width]
    return jnp.concatenate([west, array, east], axis=-1)


def vertical_mix(tracer, mixing):
    level_flux = mixing[:-1] * (tracer[:, 1:] - tracer[:, :-1])
    zero_level = jnp.zeros_like(tracer[:, :1])
    from_above = jnp.concatenate([level_flux, zero_level], axis=1)
    from_below = jnp.concatenate([zero_level, level_flux], axis=1)
    relaxation = jnp.concatenate(
        [jnp.zeros_like(tracer[:, :-1]), mixing[-1:] * tracer[:, -1:]], axis=1
    )
    return tracer + from_above - from_below - relaxation


def advect_mix(tracer, east_vel, north_vel, mixing):
    centre = tracer[..., 1:-1, 1:-1]
    vel_east = east_vel[:, 1:-1, 1:-1]
    vel_west = east_vel[:, 1:-1, :-2]
    vel_north = north_vel[:, 1:-1, 1:-1]
    vel_south = north_vel[:, :-2, 1:-1]
    flux_east = (
        jnp.maximum(vel_east, 0.0) * centre + jnp.minimum(vel_east, 0.0) * tracer[..., 1:-1, 2:]
    )
    flux_west = (
        jnp.maximum(vel_west, 0.0) * tracer[..., 1:-1, :-2] + jnp.minimum(vel_west, 0.0) * centre
    )
    flux_north = (
        jnp.maximum(vel_north, 0.0) * centre + jnp.minimum(vel_north, 0.0) * tracer[..., 2:, 1:-1]
    )
    flux_south = (
        jnp.maximum(vel_south, 0.0) * tracer[..., :-2, 1:-1] + jnp.minimum(vel_south, 0.0) * centre
    )
    advanced = centre - (flux_east - flux_west) - (flux_north - flux_south)
    return vertical_mix(advanced, mixing[:, 1:-1, 1:-1])


def to_tiles(field_grid):
    fcount, grid_rows, grid_cols = field_grid.shape
    blocks = field_grid.reshape(fcount, grid_rows, grid_cols // TILE, TILE)
    return blocks.transpose(1, 2, 0, 3).reshape(-1, fcount, TILE)


def from_tiles(tile_form, grid_rows, grid_cols):
    fcount = tile_form.shape[1]
    blocks = tile_form.reshape(grid_rows, grid_cols // TILE, fcount, TILE)
    return blocks.transpose(2, 0, 1, 3).reshape(fcount, grid_rows, grid_cols)


def bucket_places(partner_devices, owners, capacity):
    owner_list = partner_devices.reshape(-1)
    owner_hit = (owner_list[:, None] == jnp.arange(owners, dtype=jnp.int32)[None, :]).astype(
        jnp.int32
    )
    owner_rank = jnp.cumsum(owner_hit, axis=0) - owner_hit
    position = jnp.sum(owner_rank * owner_hit, axis=1)
    return owner_list * capacity + position


def advect(start, coeffs, grid_rows):
    fields = start.shape[0] * start.shape[1]
    both = jnp.concatenate([start.reshape((fields,) + start.shape[2:]), coeffs.reshape((-1,) + coeffs.shape[2:])])
    wide = wide_halo(both, NSUB)
    levels = coeffs.shape[1]
    tracer = wide[:fields].reshape(start.shape[:2] + wide.shape[1:])
    coeff_ext = wide[fields:].reshape((3, levels) + wide.shape[1:])
    rows_total = grid_rows * lax.axis_size("col")
    row_global = (
        lax.axis_index("col") * grid_rows
        + jnp.arange(grid_rows + 2 * NSUB, dtype=jnp.int32)
        - NSUB
    )
    row_open = ((row_global >= 0) & (row_global < rows_total - 1)).astype(jnp.float32)
    east_ext = coeff_ext[0]
    north_ext = coeff_ext[1] * row_open[None, :, None]
    mix_ext = coeff_ext[2]
    for step_index in range(NSUB):
        s = step_index
        e = east_ext.shape[1] - s
        w = east_ext.shape[2] - s
        tracer = advect_mix(
            tracer,
            east_ext[:, s:e, s:w],
            north_ext[:, s:e, s:w],
            mix_ext[:, s:e, s:w],
        )
    return tracer


def on_device(
    joint_tracer_field,
    courant_mixing_rates,
    oceanic_indicator,
    glacial_indicator,
    prior_oceanic_warmth,
    prior_glacial_cover,
    partner_devices,
    receiving_tile_index,
    bank_tile_entry,
    conservative_overlay_factors,
):
    owners = lax.axis_size("panel") * lax.axis_size("col")
    tile_count = partner_devices.shape[0]
    capacity = max(2, 4 * tile_count // owners)
    slots = owners * capacity
    nbank = conservative_overlay_factors.shape[0]
    on_atmos = lax.axis_index("comp") == 0
    device_tracer_share = joint_tracer_field[0]
    coeffs = courant_mixing_rates[0]
    grid_rows = coeffs.shape[2]
    grid_cols = coeffs.shape[3]
    sea_here = oceanic_indicator[0].astype(jnp.float32)
    wind_east = coeffs[0, 0]
    wind_north = coeffs[1, 0]
    airflow_speed = jnp.sqrt(wind_east * wind_east + wind_north * wind_north + 0.01)
    unfrozen_share = sea_here * (1.0 - prior_glacial_cover)
    thermal_exchange_rate = (
        2.0 * airflow_speed * (prior_oceanic_warmth - device_tracer_share[0, 0]) * unfrozen_share
    )
    evaporation_rate = (
        2.0
        * airflow_speed
        * (jnp.exp(0.1 * prior_oceanic_warmth) - device_tracer_share[1, 0])
        * unfrozen_share
    )
    heated = device_tracer_share.at[0, 0].add(thermal_exchange_rate).at[1, 0].add(evaporation_rate)
    start = jnp.where(on_atmos, heated, device_tracer_share)
    surface_flux = jnp.stack([thermal_exchange_rate, evaporation_rate])
    flux_rows = passed_along(to_tiles(surface_flux), "comp", 1).reshape(tile_count * 2, TILE)
    pairs = tile_count * 2

    bucket_place = bucket_places(partner_devices, owners, capacity)
    place_match = bucket_place[None, :] == jnp.arange(slots, dtype=jnp.int32)[:, None]
    slot_used = jnp.any(place_match, axis=1)
    slot_pair = jnp.sum(jnp.where(place_match, jnp.arange(pairs, dtype=jnp.int32)[None, :], 0), axis=1)
    slot_tile = slot_pair // 2
    slot_bank = jnp.sum(jnp.where(place_match, bank_tile_entry.reshape(-1)[None, :], 0), axis=1)

    by_bank = jnp.einsum(
        "bji,ri->brj", conservative_overlay_factors, flux_rows, precision=lax.Precision.HIGH
    ).reshape(nbank * pairs, TILE)
    f_ids = jnp.arange(2, dtype=jnp.int32)[None, :]
    slot_rows = (slot_bank * pairs + slot_tile * 2)[:, None] + f_ids
    picked = by_bank[slot_rows.reshape(-1)].reshape(slots, 2, TILE)
    buffer = jnp.where(slot_used[:, None, None], picked, 0.0).reshape(owners, capacity * 2, TILE)
    slot_label = jnp.sum(jnp.where(place_match, receiving_tile_index.reshape(-1)[None, :], 0), axis=1)
    label_row = jnp.pad(
        slot_label.reshape(owners, capacity).astype(jnp.float32), ((0, 0), (0, TILE - capacity))
    )
    bucket = jnp.concatenate([buffer, label_row[:, None, :]], axis=1)
    rows_out = capacity * 2 + 1
    arrived = lax.all_to_all(
        bucket.reshape(owners, rows_out * TILE), ("panel", "col"), 0, 0, tiled=True
    ).reshape(owners, rows_out, TILE)
    received = arrived[:, : capacity * 2].reshape(slots * 2, TILE)
    recv_slots = arrived[:, capacity * 2, :capacity].astype(jnp.int32).reshape(-1)

    row_ids = lax.broadcasted_iota(jnp.int32, (pairs, slots * 2), 0)
    col_ids = lax.broadcasted_iota(jnp.int32, (pairs, slots * 2), 1)
    recv_rep = jnp.broadcast_to(recv_slots[:, None], (slots, 2)).reshape(-1)
    slot_hit2 = (
        (recv_rep[None, :] == row_ids // 2) & (col_ids % 2 == row_ids % 2)
    ).astype(jnp.float32)
    summed = jnp.dot(slot_hit2, received, precision=lax.Precision.HIGH)
    forcing = from_tiles(summed.reshape(tile_count, 2, TILE), grid_rows, grid_cols)

    tracer = advect(start, coeffs, grid_rows)
    forced = (
        tracer.at[0, 0]
        .add(-(0.5 * sea_here * forcing[0]))
        .at[1, 0]
        .add(0.5 * sea_here * forcing[1])
    )
    new_here = jnp.where(on_atmos, tracer, forced)
    sea_temp = new_here[0, 0]
    ice_cover = (
        glacial_indicator.astype(jnp.float32) * sea_here * jnp.clip(0.5 - sea_temp, 0.0, 1.0)
    )
    ocean_surface = jnp.stack([sea_temp, ice_cover])
    ocean_tiles = to_tiles(ocean_surface).reshape(pairs, TILE)
    reply = jnp.dot(slot_hit2.T, ocean_tiles, precision=lax.Precision.HIGH).reshape(owners, capacity * 2, TILE)
    returned = lax.all_to_all(reply, ("panel", "col"), 0, 0, tiled=True).reshape(slots * 2, TILE)
    reply, late_place = lax.optimization_barrier((reply, bucket_place))
    place_rep = jnp.broadcast_to(late_place[:, None], (pairs, 2)).reshape(-1)
    p_rows = lax.broadcasted_iota(jnp.int32, (pairs * 2, slots * 2), 0)
    p_cols = lax.broadcasted_iota(jnp.int32, (pairs * 2, slots * 2), 1)
    place_hit2 = ((place_rep[:, None] == p_cols // 2) & (p_cols % 2 == p_rows % 2)).astype(
        jnp.float32
    )
    values = jnp.dot(place_hit2, returned, precision=lax.Precision.HIGH)

    by_bank_back = jnp.einsum(
        "rj,bji->bri", values, conservative_overlay_factors, precision=lax.Precision.HIGH
    ).reshape(nbank * pairs * 2, TILE)
    tile_ids = jnp.arange(tile_count, dtype=jnp.int32)[:, None]
    pair_rows = (bank_tile_entry * tile_count + tile_ids) * 4 + jnp.arange(2, dtype=jnp.int32)[None, :] * 2
    back_rows = pair_rows[:, :, None] + f_ids[:, None, :]
    numerator = jnp.sum(by_bank_back[back_rows.reshape(-1)].reshape(tile_count, 2, 2, TILE), axis=1)
    column_sums = jnp.sum(conservative_overlay_factors, axis=1)
    bank_ids = jnp.arange(nbank, dtype=jnp.int32)[None, :]
    bank_count = (bank_tile_entry[:, :1] == bank_ids).astype(jnp.float32) + (
        bank_tile_entry[:, 1:] == bank_ids
    ).astype(jnp.float32)
    denominator = jnp.dot(bank_count, column_sums, precision=lax.Precision.HIGH)
    remap_back = numerator / denominator[:, None, :]
    remapped = passed_along(from_tiles(remap_back, grid_rows, grid_cols), "comp", -1)
    surface_here = jnp.where(on_atmos, remapped, ocean_surface)
    return (new_here[None], surface_here[None])


def solution(mesh):
    return jax.shard_map(
        on_device,
        mesh=mesh,
        in_specs=(
            P("comp", None, None, "col", "panel"),
            P("comp", None, None, "col", "panel"),
            P("comp", "col", "panel"),
            P("col", "panel"),
            P("col", "panel"),
            P("col", "panel"),
            P(("panel", "col"), None),
            P(("panel", "col"), None),
            P(("panel", "col"), None),
            P(),
        ),
        out_specs=(P("comp", None, None, "col", "panel"), P("comp", None, "col", "panel")),
        check_vma=False,
    )
```
